32 devices in a mesh: rep: 16 (over z, y, core), grp: 2 (over x).
Axes of the slice: x: 2, y: 2, z: 4, core: 2. Of those that a mesh axis runs over, the one named last changes fastest.
Arguments:
- tokens: bfloat16 [4096, 1024], P(('rep', 'grp')), may hold values from -6 to 6
- cotangent: float32 [4096, 1024], P(('rep', 'grp')), may hold values from -6 to 6
- expert_index: int32 [4096, 8], P(('rep', 'grp')), may hold values from 0 to 31, as said below
- gate_weight: float32 [4096, 8], P(('rep', 'grp')), may hold values from 0.1 to 1
- attn_params: float32 [3147776], P(('rep', 'grp')), may hold values from -10 to 10
- attn_first: float32 [3147776], P(('rep', 'grp')), may hold values from -15 to 15
- attn_second: float32 [3147776], P(('rep', 'grp')), may hold values from 1 to 400
- expert_params: float32 [1572864], P(('rep', 'grp')), may hold values from -8 to 8
- expert_first: float32 [1572864], P(('rep', 'grp')), may hold values from -15 to 15
- expert_second: float32 [1572864], P(('rep', 'grp')), may hold values from 1 to 400
Outputs:
- output: float32 [4096, 1024], P(('rep', 'grp'))
- grad_tokens: float32 [4096, 1024], P(('rep', 'grp'))
- attn_grad: float32 [3147776], P(('rep', 'grp'))
- expert_grad: float32 [1572864], P(('rep', 'grp'))
- new_attn_params: float32 [3147776], P(('rep', 'grp'))
- new_attn_first: float32 [3147776], P(('rep', 'grp'))
- new_attn_second: float32 [3147776], P(('rep', 'grp'))
- new_expert_params: float32 [1572864], P(('rep', 'grp'))
- new_expert_first: float32 [1572864], P(('rep', 'grp'))
- new_expert_second: float32 [1572864], P(('rep', 'grp'))
The draws below stay inside these ranges and needn't reach their ends.
Inputs may be any that keep to these rules, and one draw needn't show every extreme that they name: `expert_index`: each row names 8 different experts. Among the 128 rows of one device, each expert below 1 is named by 8 to 32 rows, and in every draw one device has exactly 32 rows naming one of them.
All inputs are finite; a program needn't handle non-finite values.
Results may differ from the reference program's by a relative error of at most 0.012.
Values may be sent and summed in bfloat16 or wider, within the bound.
No kernel may reach another device: no remote copies, remote signals or barrier semaphores. Data moves between devices by JAX's collectives and lax.ppermute only.
A program may use at most 128 MiB of HBM per device.

```python
import math
import jax
import jax.numpy as jnp
from jax import lax

MODEL_WIDTH = 1024
QUERY_HEADS = 16
KEY_VALUE_HEADS = 8
HEAD_SIZE = 64
EXPERTS = 32
FF = 512
TOPK = 8
EXP_WIN = 1
STEP = 5
TOK_DEV = 128
PROJ = 2048
CAP = 32
TOKENS = 4096
PA = 3147776
PE = 1572864


def shuffle_rows(subkey):
    return jax.random.permutation(subkey, TOK_DEV)


def shuffle_experts(subkey):
    return jax.random.permutation(subkey, EXPERTS)


def draw_expert_index(key, part):
    block_count = TOKENS // TOK_DEV
    key_count, key_block, key_expert, key_rank, key_order = jax.random.split(key, 5)
    counts = jax.random.randint(key_count, (block_count, EXP_WIN), CAP // 4, CAP + 1)
    full_block = jax.random.randint(key_block, (), 0, block_count)
    full_expert = jax.random.randint(key_expert, (), 0, EXP_WIN)
    picked_cell = (jnp.arange(block_count)[:, None] == full_block) & (jnp.arange(EXP_WIN)[None, :] == full_expert)
    counts = jnp.where(picked_cell, CAP, counts)
    rank_keys = jax.random.split(key_rank, block_count * EXP_WIN)
    ranks = jax.vmap(shuffle_rows)(rank_keys).reshape(block_count, EXP_WIN, TOK_DEV)
    chosen = ranks < counts[:, :, None]
    chosen = jnp.transpose(chosen, (0, 2, 1)).reshape(TOKENS, EXP_WIN)
    order_keys = jax.random.split(key_order, TOKENS)
    order = jax.vmap(shuffle_experts)(order_keys).astype(jnp.int32)
    inside = jnp.arange(EXPERTS)[None, :] < EXP_WIN
    chosen_full = jnp.concatenate([chosen, jnp.zeros((TOKENS, EXPERTS - EXP_WIN), jnp.bool_)], axis=1)
    score = jnp.where(inside, jnp.where(chosen_full, order + 1000, order - 1000), order)
    top_scores, picked = lax.top_k(score, TOPK)
    return picked.astype(jnp.int32)


def draw_attn_params(key, part):
    key_gain, key_qkv, key_out = jax.random.split(key, 3)
    gains = jnp.exp(jax.random.uniform(key_gain, (2 * MODEL_WIDTH,), jnp.float32, math.log(0.1), math.log(0.5)))
    rotary_base = jnp.clip(jax.random.normal(key_qkv, (MODEL_WIDTH, PROJ), jnp.float32), -5.0, 5.0)
    outer = jnp.clip(jax.random.normal(key_out, (QUERY_HEADS * HEAD_SIZE, MODEL_WIDTH), jnp.float32), -5.0, 5.0)
    column_slice = jnp.arange(PROJ)
    column_scaling = jnp.where(column_slice < (QUERY_HEADS + KEY_VALUE_HEADS) * HEAD_SIZE, 6.0, 3.0) / math.sqrt(MODEL_WIDTH)
    qkv_part = jnp.clip(rotary_base * column_scaling[None, :], -9.5, 9.5)
    out_part = outer * 0.5
    return jnp.concatenate([gains, qkv_part.reshape(-1), out_part.reshape(-1)]).astype(jnp.float32)


def draw_expert_params(key, part):
    key_upper, key_lower = jax.random.split(key, 2)
    upper_count = EXP_WIN * MODEL_WIDTH * 2 * FF
    lower_count = EXP_WIN * FF * MODEL_WIDTH
    upper = jnp.clip(jax.random.normal(key_upper, (upper_count,), jnp.float32), -5.0, 5.0)
    lower = jnp.clip(jax.random.normal(key_lower, (lower_count,), jnp.float32), -5.0, 5.0)
    upper = upper * (4.0 / math.sqrt(MODEL_WIDTH))
    lower = lower * (8.0 / math.sqrt(FF))
    return jnp.concatenate([upper, lower]).astype(jnp.float32)


def levels(rng, extent, cuts, smallest, top_value):
    gain = 1.0
    for dim, parts in cuts:
        steps = jax.random.uniform(jax.random.fold_in(jax.random.fold_in(rng, 6), dim), (parts,), jnp.float32, smallest / len(cuts), top_value / len(cuts))
        gain = gain * jnp.repeat(jnp.exp(steps), extent[dim] // parts).reshape((-1,) + (1,) * (len(extent) - 1 - dim))
    return gain


def scatter_about(stream_key, dims, spread, bound, cuts=(), dtype=jnp.bfloat16):
    values = spread * jax.random.normal(stream_key, dims, jnp.float32)
    if cuts:
        values = values * levels(stream_key, dims, cuts, -0.22, 0.18)
    return jnp.clip(values, -bound, bound).astype(dtype)


def setup_inputs(seed: int = 0) -> dict:
    seeds = jax.random.split(jax.random.key(seed), 11)
    tokens = scatter_about(seeds[0], (TOKENS, MODEL_WIDTH), 1.0, 6.0, ((0, 32),))
    cotangent = scatter_about(seeds[1], (TOKENS, MODEL_WIDTH), 1.0, 6.0, ((0, 32),), jnp.float32)
    expert_index = draw_expert_index(jax.random.fold_in(seeds[10], 71), 0)
    gate_weight = jnp.clip(jnp.exp(math.log(1.0) - 2.3025851 * jax.random.uniform(seeds[3], (TOKENS, TOPK), jnp.float32) ** levels(seeds[3], (TOKENS, TOPK), ((0, 32),), -0.2, 0.2)), 0.1, 1.0)
    attn_params = draw_attn_params(jax.random.fold_in(seeds[10], 71), 0)
    attn_first = scatter_about(seeds[5], (PA,), 3.0, 15.0, ((0, 32),), jnp.float32)
    attn_second = jnp.clip(jnp.exp(math.log(400.0) - 5.9914645 * jax.random.uniform(seeds[6], (PA,), jnp.float32) ** levels(seeds[6], (PA,), ((0, 32),), -0.2, 0.2)), 1.0, 400.0)
    expert_params = draw_expert_params(jax.random.fold_in(seeds[10], 71), 0)
    expert_first = scatter_about(seeds[8], (PE,), 3.0, 15.0, ((0, 32),), jnp.float32)
    expert_second = jnp.clip(jnp.exp(math.log(400.0) - 5.9914645 * jax.random.uniform(seeds[9], (PE,), jnp.float32) ** levels(seeds[9], (PE,), ((0, 32),), -0.2, 0.2)), 1.0, 400.0)
    return dict(tokens=tokens, cotangent=cotangent, expert_index=expert_index, gate_weight=gate_weight, attn_params=attn_params, attn_first=attn_first, attn_second=attn_second, expert_params=expert_params, expert_first=expert_first, expert_second=expert_second)


NORM_EPS = 1e-06
ROPE_BASE = 10000.0
ATTN_MULT = 0.015625
RESID_MULT = 0.22
LEARN_RATE = 0.05
BETA_ONE = 0.9
BETA_TWO = 0.95
ADAM_EPS = 1e-08
DECAY = 0.1

def unpack_attention(flat_vec):
    start_qkv = 2 * MODEL_WIDTH
    start_out = 2 * MODEL_WIDTH + MODEL_WIDTH * PROJ
    return (flat_vec[:MODEL_WIDTH], flat_vec[MODEL_WIDTH:start_qkv], flat_vec[start_qkv:start_out].reshape(MODEL_WIDTH, PROJ), flat_vec[start_out:].reshape(QUERY_HEADS * HEAD_SIZE, MODEL_WIDTH))

def unpack_experts(flat_vec):
    split_at = EXP_WIN * MODEL_WIDTH * 2 * FF
    return (flat_vec[:split_at].reshape(EXP_WIN, MODEL_WIDTH, 2 * FF), flat_vec[split_at:].reshape(EXP_WIN, FF, MODEL_WIDTH))

def rope_tables(sequence_length):
    half_width = HEAD_SIZE // 2
    frequency = ROPE_BASE ** (-(jnp.arange(half_width).astype(jnp.float32) * 2.0) / HEAD_SIZE)
    angles = jnp.arange(sequence_length).astype(jnp.float32)[:, None] * frequency[None, :]
    cos_table = jnp.concatenate([jnp.cos(angles), jnp.cos(angles)], axis=1)
    sin_table = jnp.concatenate([jnp.sin(angles), jnp.sin(angles)], axis=1)
    return (cos_table[:, None, :], sin_table[:, None, :])

def rotate_half(values):
    half_width = values.shape[-1] // 2
    return jnp.concatenate([-values[..., half_width:], values[..., :half_width]], axis=-1)

def apply_rope(values, cos_table, sin_table):
    return values * cos_table + rotate_half(values) * sin_table

def undo_rope(grads_in, cos_table, sin_table):
    return grads_in * cos_table - rotate_half(grads_in * sin_table)

def rms_forward(values, gain_vec):
    inv_rms = lax.rsqrt(lax.optimization_barrier(jnp.mean(values * values, axis=-1, keepdims=True)) + NORM_EPS)
    return (values * inv_rms * gain_vec, inv_rms)

def rms_backward(values, inv_rms, gain_vec, grad_normed):
    weighted = grad_normed * gain_vec
    grad_values = inv_rms * weighted - values * (inv_rms * inv_rms * inv_rms) * lax.optimization_barrier(jnp.mean(weighted * values, axis=-1, keepdims=True))
    grad_gain = lax.optimization_barrier(jnp.sum(grad_normed * values * inv_rms, axis=0))
    return (grad_values, grad_gain)

def route_tables(index_rows, gate_rows):
    experts_here = jnp.arange(EXP_WIN).astype(jnp.int32)
    matches = index_rows[:, :, None] == experts_here[None, None, :]
    member = jnp.any(matches, axis=1)
    weight = lax.optimization_barrier(jnp.sum(jnp.where(matches, gate_rows[:, :, None], 0.0), axis=1))
    position = jnp.cumsum(member.astype(jnp.int32), axis=0) - 1
    slot_index = jnp.where(member, position, CAP).astype(jnp.int32)
    dispatch = jnp.transpose(slot_index)[:, None, :] == jnp.arange(CAP).astype(jnp.int32)[None, :, None]
    return (member, weight, slot_index, dispatch)

def layer_pass(seq_rows, cot_rows, index_rows, gate_rows, weights):
    gain_one, gain_two, w_qkv, w_out, w_gate_up, w_down = weights
    single_float = jnp.float32
    sequence_length = seq_rows.shape[0]
    heads_per_group = QUERY_HEADS // KEY_VALUE_HEADS
    gain_one_f = gain_one.astype(single_float)
    gain_two_f = gain_two.astype(single_float)
    inputs = seq_rows.astype(single_float)
    normed_one, scale_one = rms_forward(inputs, gain_one_f)
    normed_one = normed_one.astype(jnp.bfloat16)
    query_key_value = jnp.dot(normed_one, w_qkv, preferred_element_type=single_float)
    query = query_key_value[:, :QUERY_HEADS * HEAD_SIZE].reshape(sequence_length, QUERY_HEADS, HEAD_SIZE)
    unrotated_keys = query_key_value[:, QUERY_HEADS * HEAD_SIZE:(QUERY_HEADS + KEY_VALUE_HEADS) * HEAD_SIZE].reshape(sequence_length, KEY_VALUE_HEADS, HEAD_SIZE)
    projected_value = query_key_value[:, (QUERY_HEADS + KEY_VALUE_HEADS) * HEAD_SIZE:].reshape(sequence_length, KEY_VALUE_HEADS, HEAD_SIZE)
    cos_table, sin_table = rope_tables(sequence_length)
    rotated_query = apply_rope(query, cos_table, sin_table).astype(jnp.bfloat16)
    keys_rot = apply_rope(unrotated_keys, cos_table, sin_table).astype(jnp.bfloat16)
    value_low = projected_value.astype(jnp.bfloat16)
    query_float = rotated_query.reshape(sequence_length, KEY_VALUE_HEADS, heads_per_group, HEAD_SIZE).astype(single_float)
    keys_f = keys_rot.astype(single_float)
    value_f = value_low.astype(single_float)
    scores = jnp.einsum('tkgd,skd->kgts', query_float, keys_f) * ATTN_MULT
    causal = jnp.arange(sequence_length)[:, None] >= jnp.arange(sequence_length)[None, :]
    scores = jnp.where(causal, scores, -jnp.inf)
    top_score = lax.optimization_barrier(jnp.max(scores, axis=-1, keepdims=True))
    log_total = top_score + jnp.log(lax.optimization_barrier(jnp.sum(jnp.exp(scores - top_score), axis=-1, keepdims=True)))
    prob_f = jnp.exp(scores - log_total)
    probs_low = prob_f.astype(jnp.bfloat16)
    attention_output = jnp.einsum('kgts,skd->tkgd', probs_low.astype(single_float), value_f)
    attention_output = attention_output.reshape(sequence_length, QUERY_HEADS * HEAD_SIZE).astype(jnp.bfloat16)
    hidden = inputs + RESID_MULT * jnp.dot(attention_output, w_out, preferred_element_type=single_float)
    normed_two, scale_two = rms_forward(hidden, gain_two_f)
    normed_two = normed_two.astype(jnp.bfloat16)
    member, weight, slot_index, dispatch = route_tables(index_rows, gate_rows)
    dispatch_f = dispatch.astype(single_float)
    blocks = jnp.einsum('ect,td->ecd', dispatch_f, normed_two.astype(single_float)).astype(jnp.bfloat16)
    gate_up = jnp.einsum('ecd,edf->ecf', blocks.astype(single_float), w_gate_up.astype(single_float))
    gate_part = gate_up[..., :FF]
    up_part = gate_up[..., FF:]
    sigma = jax.nn.sigmoid(gate_part)
    activated = (gate_part * sigma * up_part).astype(jnp.bfloat16)
    expert_out = jnp.einsum('ecf,efd->ecd', activated.astype(single_float), w_down.astype(single_float))
    clipped = jnp.minimum(slot_index, CAP - 1)
    mixture = jnp.zeros_like(hidden)
    for expert in range(EXP_WIN):
        mixture = mixture + weight[:, expert:expert + 1] * jnp.take(expert_out[expert], clipped[:, expert], axis=0)
    output = hidden + RESID_MULT * mixture
    grad_mix = RESID_MULT * cot_rows
    scaled = jnp.transpose(weight)[:, :, None] * grad_mix[None, :, :]
    grad_blocks = jnp.einsum('ect,etd->ecd', dispatch_f, scaled, precision=lax.Precision.HIGHEST).astype(jnp.bfloat16)
    grad_blocks_f = grad_blocks.astype(single_float)
    grad_w_down = jnp.einsum('ecf,ecd->efd', activated.astype(single_float), grad_blocks_f)
    grad_act = jnp.einsum('ecd,efd->ecf', grad_blocks_f, w_down.astype(single_float))
    silu_slope = sigma * (1.0 + gate_part * (1.0 - sigma))
    grad_gate_up = jnp.concatenate([grad_act * up_part * silu_slope, grad_act * gate_part * sigma], axis=-1).astype(jnp.bfloat16)
    grad_w_gate_up = jnp.einsum('ecd,ecf->edf', blocks.astype(single_float), grad_gate_up.astype(single_float))
    grad_in_blocks = jnp.einsum('ecf,edf->ecd', grad_gate_up.astype(single_float), w_gate_up.astype(single_float))
    grad_normed_two = jnp.zeros_like(hidden)
    for expert in range(EXP_WIN):
        grad_normed_two = grad_normed_two + member[:, expert:expert + 1].astype(single_float) * jnp.take(grad_in_blocks[expert], clipped[:, expert], axis=0)
    grad_hidden_n, grad_gain_two = rms_backward(hidden, scale_two, gain_two_f, grad_normed_two)
    grad_hidden = cot_rows + grad_hidden_n
    grad_branch = (RESID_MULT * grad_hidden).astype(jnp.bfloat16)
    grad_w_out = jnp.dot(attention_output.T, grad_branch, preferred_element_type=single_float)
    attention_output_gradient = jnp.dot(grad_branch, w_out.T, preferred_element_type=single_float).astype(jnp.bfloat16)
    attention_gradient_float = attention_output_gradient.reshape(sequence_length, KEY_VALUE_HEADS, heads_per_group, HEAD_SIZE).astype(single_float)
    attention_output_float = attention_output.reshape(sequence_length, KEY_VALUE_HEADS, heads_per_group, HEAD_SIZE).astype(single_float)
    delta = jnp.transpose(lax.optimization_barrier(jnp.sum(attention_gradient_float * attention_output_float, axis=-1)), (1, 2, 0))
    grad_probs = jnp.einsum('tkgd,skd->kgts', attention_gradient_float, value_f)
    grad_scores = (prob_f * (grad_probs - delta[..., None]) * ATTN_MULT).astype(jnp.bfloat16)
    grad_scores_f = grad_scores.astype(single_float)
    value_gradient = jnp.einsum('kgts,tkgd->skd', probs_low.astype(single_float), attention_gradient_float)
    query_gradient = jnp.einsum('kgts,skd->tkgd', grad_scores_f, keys_f).reshape(sequence_length, QUERY_HEADS, HEAD_SIZE)
    key_gradient = jnp.einsum('kgts,tkgd->skd', grad_scores_f, query_float)
    query_gradient = undo_rope(query_gradient, cos_table, sin_table)
    key_gradient = undo_rope(key_gradient, cos_table, sin_table)
    query_key_value_gradient = jnp.concatenate([query_gradient.reshape(sequence_length, QUERY_HEADS * HEAD_SIZE), key_gradient.reshape(sequence_length, KEY_VALUE_HEADS * HEAD_SIZE), value_gradient.reshape(sequence_length, KEY_VALUE_HEADS * HEAD_SIZE)], axis=1).astype(jnp.bfloat16)
    grad_w_qkv = jnp.dot(normed_one.T, query_key_value_gradient, preferred_element_type=single_float)
    grad_normed_one = jnp.dot(query_key_value_gradient, w_qkv.T, preferred_element_type=single_float)
    grad_inputs_n, grad_gain_one = rms_backward(inputs, scale_one, gain_one_f, grad_normed_one)
    grad_inputs = grad_hidden + grad_inputs_n
    return (output, grad_inputs, (grad_gain_one, grad_gain_two, grad_w_qkv, grad_w_out, grad_w_gate_up, grad_w_down))

def adamw(current, gradient, moment_one, moment_two):
    moment_one_new = BETA_ONE * moment_one + (1.0 - BETA_ONE) * gradient
    moment_two_new = BETA_TWO * moment_two + (1.0 - BETA_TWO) * gradient * gradient
    first_hat = moment_one_new / (1.0 - BETA_ONE ** STEP)
    second_hat = moment_two_new / (1.0 - BETA_TWO ** STEP)
    updated = current - LEARN_RATE * (first_hat / (jnp.sqrt(second_hat) + ADAM_EPS) + DECAY * current)
    return (updated, moment_one_new, moment_two_new)

def reference(tokens, cotangent, expert_index, gate_weight, attn_params, attn_first, attn_second, expert_params, expert_first, expert_second):
    weights = unpack_attention(attn_params.astype(jnp.bfloat16)) + unpack_experts(expert_params.astype(jnp.bfloat16))
    seq_count = TOKENS // TOK_DEV
    sequences = (tokens.reshape(seq_count, TOK_DEV, MODEL_WIDTH), cotangent.reshape(seq_count, TOK_DEV, MODEL_WIDTH), expert_index.reshape(seq_count, TOK_DEV, TOPK), gate_weight.reshape(seq_count, TOK_DEV, TOPK))
    running = tuple((jnp.zeros(piece.shape, jnp.float32) for piece in weights))

    def per_sequence(totals, pieces):
        output, grad_inputs, grad_list = layer_pass(pieces[0], pieces[1], pieces[2], pieces[3], weights)
        return (tuple((accum + gradient for accum, gradient in zip(totals, grad_list))), (output, grad_inputs))
    grad_sums, (outputs, grad_rows) = lax.scan(per_sequence, running, sequences)
    attn_grad = jnp.concatenate([grad_sums[0], grad_sums[1], grad_sums[2].reshape(-1), grad_sums[3].reshape(-1)])
    expert_grad = jnp.concatenate([grad_sums[4].reshape(-1), grad_sums[5].reshape(-1)])
    new_attn, new_attn_first, new_attn_second = adamw(attn_params, attn_grad, attn_first, attn_second)
    new_expert, new_expert_first, new_expert_second = adamw(expert_params, expert_grad, expert_first, expert_second)
    return (outputs.reshape(TOKENS, MODEL_WIDTH), grad_rows.reshape(TOKENS, MODEL_WIDTH), attn_grad, expert_grad, new_attn, new_attn_first, new_attn_second, new_expert, new_expert_first, new_expert_second)
```

```python
import jax
import jax.numpy as jnp
from jax import lax
from jax.sharding import PartitionSpec as P

MODEL_WIDTH = 1024
QUERY_HEADS = 16
KEY_VALUE_HEADS = 8
HEAD_SIZE = 64
FF = 512
EXP_WIN = 1
STEP = 5
PROJ = 2048
CAP = 32


NORM_EPS = 1e-06
ROPE_BASE = 10000.0
ATTN_MULT = 0.015625
RESID_MULT = 0.22
LEARN_RATE = 0.05
BETA_ONE = 0.9
BETA_TWO = 0.95
ADAM_EPS = 1e-08
DECAY = 0.1


STREAMS = 3


def to_rows(flat_vec, offset, rows):
    room = jnp.zeros(((rows + 1) * PROJ,), flat_vec.dtype)
    return lax.dynamic_update_slice(room, flat_vec, (offset,)).reshape(rows + 1, PROJ)


def bits_of(name, count):
    return [(name, 1 << k) for k in reversed(range(count.bit_length() - 1))]


def stage_orders(rep_count, grp_count):
    dims = bits_of("rep", rep_count)[:-1] + bits_of("grp", grp_count)
    head, tail = dims[:-STREAMS], dims[-STREAMS:]
    return [head + tail[i:] + tail[:i] + [("rep", 1)] for i in range(STREAMS)]


def swap(piece, dim):
    name, bit = dim
    count = lax.axis_size(name)
    return lax.ppermute(piece, name, [(i, i ^ bit) for i in range(count)])


def my_bit(dim):
    name, bit = dim
    return (lax.axis_index(name) // bit) % 2


def in_order(mine, other, bit):
    room = jnp.zeros((2,) + mine.shape, mine.dtype)
    start = (0,) * mine.ndim
    room = lax.dynamic_update_slice(room, mine[None], (bit,) + start)
    return lax.dynamic_update_slice(room, other[None], (1 - bit,) + start)


def gather_streams(streams, rep_count, grp_count):
    orders = stage_orders(rep_count, grp_count)
    for stage in range(len(orders[0])):
        others = [swap(piece, order[stage]) for piece, order in zip(streams, orders)]
        streams, others = lax.optimization_barrier((streams, others))
        streams = [
            in_order(piece, other, my_bit(order[stage]))
            for piece, other, order in zip(streams, others, orders)
        ]
    canonical = bits_of("rep", rep_count) + bits_of("grp", grp_count)
    out = []
    for piece, order in zip(streams, orders):
        axes = [len(order) - 1 - order.index(dim) for dim in canonical]
        piece = jnp.transpose(piece, axes + [len(order), len(order) + 1])
        out.append(piece.reshape((rep_count * grp_count,) + piece.shape[-2:]))
    return out


def reduce_streams(streams, rep_count, grp_count):
    orders = [list(reversed(order)) for order in stage_orders(rep_count, grp_count)]
    dims = bits_of("rep", rep_count) + bits_of("grp", grp_count)
    streams = [piece.reshape((2,) * len(dims) + piece.shape[1:]) for piece in streams]
    left = [list(dims) for _ in streams]
    for stage in range(len(dims)):
        kept, others = [], []
        for i, piece in enumerate(streams):
            dim = orders[i][stage]
            axis = left[i].index(dim)
            left[i].pop(axis)
            bit = my_bit(dim)
            kept.append(lax.dynamic_index_in_dim(piece, bit, axis, keepdims=False))
            others.append(
                swap(lax.dynamic_index_in_dim(piece, 1 - bit, axis, keepdims=False), dim)
            )
        kept, others = lax.optimization_barrier((kept, others))
        streams = [
            mine.astype(jnp.float32) + other.astype(jnp.float32)
            for mine, other in zip(kept, others)
        ]
        if stage + 1 < len(dims):
            streams = [piece.astype(jnp.bfloat16) for piece in streams]
    return streams


def rope_tables(sequence_length):
    half_width = HEAD_SIZE // 2
    frequency = ROPE_BASE ** (-(jnp.arange(half_width).astype(jnp.float32) * 2.0) / HEAD_SIZE)
    angles = jnp.arange(sequence_length).astype(jnp.float32)[:, None] * frequency[None, :]
    cos_table = jnp.concatenate([jnp.cos(angles), jnp.cos(angles)], axis=1)
    sin_table = jnp.concatenate([jnp.sin(angles), jnp.sin(angles)], axis=1)
    return (cos_table[:, None, :], sin_table[:, None, :])


def rotate_half(values):
    half_width = values.shape[-1] // 2
    return jnp.concatenate([-values[..., half_width:], values[..., :half_width]], axis=-1)


def apply_rope(values, cos_table, sin_table):
    return values * cos_table + rotate_half(values) * sin_table


def undo_rope(grads_in, cos_table, sin_table):
    return grads_in * cos_table - rotate_half(grads_in * sin_table)


def rms_forward(values, gain_vec):
    inv_rms = lax.rsqrt(jnp.mean(values * values, axis=-1, keepdims=True) + NORM_EPS)
    return (values * inv_rms * gain_vec, inv_rms)


def rms_backward(values, inv_rms, gain_vec, grad_normed):
    weighted = grad_normed * gain_vec
    grad_values = inv_rms * weighted - values * (inv_rms * inv_rms * inv_rms) * jnp.mean(
        weighted * values, axis=-1, keepdims=True
    )
    grad_gain = jnp.sum(grad_normed * values * inv_rms, axis=0)
    return (grad_values, grad_gain)


def route_tables(index_rows, gate_rows):
    experts_here = jnp.arange(EXP_WIN)
    matches = index_rows[:, :, None] == experts_here[None, None, :]
    member = jnp.any(matches, axis=1)
    weight = jnp.sum(jnp.where(matches, gate_rows[:, :, None], 0.0), axis=1)
    position = jnp.cumsum(member.astype(jnp.int32), axis=0) - 1
    slot_index = jnp.where(member, position, CAP)
    dispatch = jnp.transpose(slot_index)[:, None, :] == jnp.arange(CAP)[None, :, None]
    return (member, weight, slot_index, dispatch)


def causal_scores(rotated_query, keys_rot):
    sequence_length = rotated_query.shape[0]
    scores = (
        jnp.einsum("tgd,sd->gts", rotated_query, keys_rot, preferred_element_type=jnp.float32)
        * ATTN_MULT
    )
    causal = lax.broadcasted_iota(
        jnp.int32, (sequence_length, sequence_length), 0
    ) >= lax.broadcasted_iota(jnp.int32, (sequence_length, sequence_length), 1)
    return jnp.where(causal[None], scores, -jnp.inf)


def head_forward(pieces):
    rotated_query, keys_rot, value_low = pieces
    scores = causal_scores(rotated_query, keys_rot)
    top_score = jnp.max(scores, axis=-1, keepdims=True)
    log_total = top_score + jnp.log(jnp.sum(jnp.exp(scores - top_score), axis=-1, keepdims=True))
    probs_low = jnp.exp(scores - log_total).astype(jnp.bfloat16)
    attention_output = jnp.einsum(
        "gts,sd->tgd", probs_low, value_low, preferred_element_type=jnp.float32
    )
    return (attention_output.astype(jnp.bfloat16), log_total)


def head_backward(pieces):
    rotated_query, keys_rot, value_low, attention_output, grad_att, log_total = pieces
    scores = causal_scores(rotated_query, keys_rot)
    prob_f = jnp.exp(scores - log_total)
    probs_low = prob_f.astype(jnp.bfloat16)
    delta = jnp.sum(grad_att.astype(jnp.float32) * attention_output.astype(jnp.float32), axis=-1)
    grad_probs = jnp.einsum("tgd,sd->gts", grad_att, value_low, preferred_element_type=jnp.float32)
    grad_scores = (prob_f * (grad_probs - jnp.transpose(delta)[:, :, None]) * ATTN_MULT).astype(
        jnp.bfloat16
    )
    value_gradient = jnp.einsum(
        "gts,tgd->sd", probs_low, grad_att, preferred_element_type=jnp.float32
    )
    query_gradient = jnp.einsum(
        "gts,sd->tgd", grad_scores, keys_rot, preferred_element_type=jnp.float32
    )
    key_gradient = jnp.einsum(
        "gts,tgd->sd", grad_scores, rotated_query, preferred_element_type=jnp.float32
    )
    return (query_gradient, key_gradient, value_gradient)


def adamw(current, gradient, moment_one, moment_two):
    moment_one_new = BETA_ONE * moment_one + (1.0 - BETA_ONE) * gradient
    moment_two_new = BETA_TWO * moment_two + (1.0 - BETA_TWO) * gradient * gradient
    first_hat = moment_one_new / (1.0 - BETA_ONE**STEP)
    second_hat = moment_two_new / (1.0 - BETA_TWO**STEP)
    updated = current - LEARN_RATE * (
        first_hat / (jnp.sqrt(second_hat) + ADAM_EPS) + DECAY * current
    )
    return (updated, moment_one_new, moment_two_new)


def per_device(
    tokens,
    cotangent,
    expert_index,
    gate_weight,
    attn_params,
    attn_first,
    attn_second,
    expert_params,
    expert_first,
    expert_second,
):
    single_float = jnp.float32
    rep_count = lax.axis_size("rep")
    grp_count = lax.axis_size("grp")
    device_count = rep_count * grp_count
    me = lax.axis_index("rep") * grp_count + lax.axis_index("grp")
    rows = attn_params.shape[0] // PROJ
    extra = attn_params.shape[0] - rows * PROJ
    part_rows = rows // STREAMS
    attn_rows = to_rows(attn_params.astype(jnp.bfloat16), extra * me, rows)
    expert_rows = expert_params.astype(jnp.bfloat16).reshape(rows, MODEL_WIDTH)
    tail_tile = attn_rows[rows].reshape(part_rows, PROJ // part_rows)
    both = jnp.concatenate([attn_rows[:rows], expert_rows], axis=1).reshape(
        STREAMS, part_rows, PROJ + MODEL_WIDTH
    )
    streams = [jnp.concatenate([both[0], tail_tile], axis=1)] + [both[i] for i in range(1, STREAMS)]
    streams = gather_streams(streams, rep_count, grp_count)
    tails = streams[0][:, :, PROJ + MODEL_WIDTH :].reshape(device_count, PROJ)
    main = jnp.stack([piece[:, :, :PROJ] for piece in streams], axis=1)
    main = main.reshape(device_count, rows, PROJ)
    first_rows = main[1:, :1] + tails[:-1, None]
    main = lax.dynamic_update_slice(main, first_rows, (1, 0, 0)).reshape(device_count * rows, PROJ)
    experts = jnp.stack(
        [piece[:, :, PROJ : PROJ + MODEL_WIDTH] for piece in streams], axis=1
    ).reshape(device_count * rows, MODEL_WIDTH)
    gain_one = main[0, :MODEL_WIDTH]
    gain_two = main[0, MODEL_WIDTH:]
    w_qkv = main[1 : MODEL_WIDTH + 1]
    w_out = jnp.concatenate([main[MODEL_WIDTH + 1 :], tails[-1:]], axis=0).reshape(
        QUERY_HEADS * HEAD_SIZE, MODEL_WIDTH
    )
    w_gate_up = experts[:MODEL_WIDTH].reshape(1, MODEL_WIDTH, 2 * FF)
    w_down = experts[MODEL_WIDTH:].reshape(1, FF, MODEL_WIDTH)
    sequence_length = tokens.shape[0]
    heads_per_group = QUERY_HEADS // KEY_VALUE_HEADS
    gain_one_f = gain_one.astype(single_float)
    gain_two_f = gain_two.astype(single_float)
    inputs = tokens.astype(single_float)
    normed_one, scale_one = rms_forward(inputs, gain_one_f)
    normed_one = normed_one.astype(jnp.bfloat16)
    query_key_value = jnp.dot(normed_one, w_qkv, preferred_element_type=single_float)
    query = query_key_value[:, : QUERY_HEADS * HEAD_SIZE].reshape(
        sequence_length, QUERY_HEADS, HEAD_SIZE
    )
    unrotated_keys = query_key_value[
        :, QUERY_HEADS * HEAD_SIZE : (QUERY_HEADS + KEY_VALUE_HEADS) * HEAD_SIZE
    ].reshape(sequence_length, KEY_VALUE_HEADS, HEAD_SIZE)
    projected_value = query_key_value[:, (QUERY_HEADS + KEY_VALUE_HEADS) * HEAD_SIZE :].reshape(
        sequence_length, KEY_VALUE_HEADS, HEAD_SIZE
    )
    cos_table, sin_table = rope_tables(sequence_length)
    rotated_query = apply_rope(query, cos_table, sin_table).astype(jnp.bfloat16)
    keys_rot = apply_rope(unrotated_keys, cos_table, sin_table).astype(jnp.bfloat16)
    value_low = projected_value.astype(jnp.bfloat16)
    query_per_head = jnp.transpose(
        rotated_query.reshape(sequence_length, KEY_VALUE_HEADS, heads_per_group, HEAD_SIZE),
        (1, 0, 2, 3),
    )
    keys_heads = jnp.transpose(keys_rot, (1, 0, 2))
    value_heads = jnp.transpose(value_low, (1, 0, 2))
    attended_heads, log_totals = lax.map(head_forward, (query_per_head, keys_heads, value_heads))
    attention_output = jnp.transpose(attended_heads, (1, 0, 2, 3)).reshape(
        sequence_length, QUERY_HEADS * HEAD_SIZE
    )
    hidden = inputs + RESID_MULT * jnp.dot(
        attention_output, w_out, preferred_element_type=single_float
    )
    normed_two, scale_two = rms_forward(hidden, gain_two_f)
    normed_two = normed_two.astype(jnp.bfloat16)
    member, weight, slot_index, dispatch = route_tables(expert_index, gate_weight)
    blocks = jnp.einsum(
        "ect,td->ecd",
        dispatch.astype(jnp.bfloat16),
        normed_two,
        preferred_element_type=single_float,
    ).astype(jnp.bfloat16)
    gate_up = jnp.einsum("ecd,edf->ecf", blocks, w_gate_up, preferred_element_type=single_float)
    gate_part = gate_up[..., :FF]
    up_part = gate_up[..., FF:]
    sigma = jax.nn.sigmoid(gate_part)
    activated = (gate_part * sigma * up_part).astype(jnp.bfloat16)
    expert_out = jnp.einsum("ecf,efd->ecd", activated, w_down, preferred_element_type=single_float)
    clipped = jnp.minimum(slot_index, CAP - 1)
    expert = 0
    mixture = weight * jnp.take(expert_out[expert], clipped[:, expert], axis=0)
    output = hidden + RESID_MULT * mixture
    grad_mix = RESID_MULT * cotangent
    scaled = jnp.transpose(weight)[:, :, None] * grad_mix[None, :, :]
    grad_blocks = jnp.einsum(
        "ect,etd->ecd", dispatch.astype(single_float), scaled, precision=lax.Precision.HIGHEST
    ).astype(jnp.bfloat16)
    grad_w_down = jnp.einsum(
        "ecf,ecd->efd", activated, grad_blocks, preferred_element_type=single_float
    )
    grad_act = jnp.einsum("ecd,efd->ecf", grad_blocks, w_down, preferred_element_type=single_float)
    silu_slope = sigma * (1.0 + gate_part * (1.0 - sigma))
    grad_gate_up = jnp.concatenate(
        [grad_act * up_part * silu_slope, grad_act * gate_part * sigma], axis=-1
    ).astype(jnp.bfloat16)
    grad_w_gate_up = jnp.einsum(
        "ecd,ecf->edf", blocks, grad_gate_up, preferred_element_type=single_float
    )
    expert_grad_rows = jnp.concatenate(
        [grad_w_gate_up.reshape(MODEL_WIDTH, 2 * FF), grad_w_down.reshape(FF, MODEL_WIDTH)]
    ).astype(jnp.bfloat16)
    grad_in_blocks = jnp.einsum(
        "ecf,edf->ecd", grad_gate_up, w_gate_up, preferred_element_type=single_float
    )
    expert = 0
    grad_normed_two = member.astype(single_float) * jnp.take(
        grad_in_blocks[expert], clipped[:, expert], axis=0
    )
    grad_hidden_n, grad_gain_two = rms_backward(hidden, scale_two, gain_two_f, grad_normed_two)
    grad_hidden = cotangent + grad_hidden_n
    grad_branch = (RESID_MULT * grad_hidden).astype(jnp.bfloat16)
    grad_w_out = jnp.einsum(
        "ti,tj->ij", attention_output, grad_branch, preferred_element_type=single_float
    )
    attention_output_gradient = jnp.einsum(
        "tj,ij->ti", grad_branch, w_out, preferred_element_type=single_float
    ).astype(jnp.bfloat16)
    attention_gradient_heads = jnp.transpose(
        attention_output_gradient.reshape(
            sequence_length, KEY_VALUE_HEADS, heads_per_group, HEAD_SIZE
        ),
        (1, 0, 2, 3),
    )
    grad_query_h, grad_keys_h, grad_value_h = lax.map(
        head_backward,
        (
            query_per_head,
            keys_heads,
            value_heads,
            attended_heads,
            attention_gradient_heads,
            log_totals,
        ),
    )
    query_gradient = jnp.transpose(grad_query_h, (1, 0, 2, 3)).reshape(
        sequence_length, QUERY_HEADS, HEAD_SIZE
    )
    key_gradient = jnp.transpose(grad_keys_h, (1, 0, 2))
    value_gradient = jnp.transpose(grad_value_h, (1, 0, 2))
    query_gradient = undo_rope(query_gradient, cos_table, sin_table)
    key_gradient = undo_rope(key_gradient, cos_table, sin_table)
    query_key_value_gradient = jnp.concatenate(
        [
            query_gradient.reshape(sequence_length, QUERY_HEADS * HEAD_SIZE),
            key_gradient.reshape(sequence_length, KEY_VALUE_HEADS * HEAD_SIZE),
            value_gradient.reshape(sequence_length, KEY_VALUE_HEADS * HEAD_SIZE),
        ],
        axis=1,
    ).astype(jnp.bfloat16)
    grad_w_qkv = jnp.einsum(
        "ti,tj->ij", normed_one, query_key_value_gradient, preferred_element_type=single_float
    )
    grad_normed_one = jnp.einsum(
        "tj,ij->ti", query_key_value_gradient, w_qkv, preferred_element_type=single_float
    )
    grad_inputs_n, grad_gain_one = rms_backward(inputs, scale_one, gain_one_f, grad_normed_one)
    grad_tokens = grad_hidden + grad_inputs_n
    gain_row = jnp.concatenate([grad_gain_one, grad_gain_two]).reshape(1, PROJ)
    attn_grad_rows = jnp.concatenate(
        [gain_row, grad_w_qkv, grad_w_out.reshape(-1, PROJ)]
    ).astype(jnp.bfloat16)
    tail_rows = attn_grad_rows[rows::rows].reshape(device_count, part_rows, PROJ // part_rows)
    attn_windows = attn_grad_rows[:-1].reshape(device_count, STREAMS, part_rows, PROJ)
    expert_windows = expert_grad_rows.reshape(device_count, STREAMS, part_rows, MODEL_WIDTH)
    both = jnp.concatenate([attn_windows, expert_windows], axis=3)
    streams = [jnp.concatenate([both[:, 0], tail_rows], axis=2)] + [
        both[:, i] for i in range(1, STREAMS)
    ]
    streams = reduce_streams(streams, rep_count, grp_count)
    tail_owned = streams[0][:, PROJ + MODEL_WIDTH :].reshape(1, PROJ)
    attn_owned = jnp.concatenate([piece[:, :PROJ] for piece in streams] + [tail_owned])
    attn_grad = lax.dynamic_slice(
        attn_owned.reshape(-1), (extra * me,), (attn_params.shape[0],)
    )
    expert_grad = jnp.concatenate(
        [piece[:, PROJ : PROJ + MODEL_WIDTH] for piece in streams]
    ).reshape(-1)
    new_attn, new_attn_first, new_attn_second = adamw(
        attn_params, attn_grad, attn_first, attn_second
    )
    new_expert, new_expert_first, new_expert_second = adamw(
        expert_params, expert_grad, expert_first, expert_second
    )
    return (
        output,
        grad_tokens,
        attn_grad,
        expert_grad,
        new_attn,
        new_attn_first,
        new_attn_second,
        new_expert,
        new_expert_first,
        new_expert_second,
    )


def solution(mesh):
    in_specs = (
        P(("rep", "grp"), None),
        P(("rep", "grp"), None),
        P(("rep", "grp"), None),
        P(("rep", "grp"), None),
        P(("rep", "grp")),
        P(("rep", "grp")),
        P(("rep", "grp")),
        P(("rep", "grp")),
        P(("rep", "grp")),
        P(("rep", "grp")),
    )
    out_specs = (
        P(("rep", "grp"), None),
        P(("rep", "grp"), None),
        P(("rep", "grp")),
        P(("rep", "grp")),
        P(("rep", "grp")),
        P(("rep", "grp")),
        P(("rep", "grp")),
        P(("rep", "grp")),
        P(("rep", "grp")),
        P(("rep", "grp")),
    )
    return jax.shard_map(
        per_device, mesh=mesh, in_specs=in_specs, out_specs=out_specs, check_vma=False
    )
```

```python
from functools import partial

import jax
import jax.numpy as jnp
from jax import lax
from jax.experimental import pallas as pl
from jax.experimental.pallas import tpu as pltpu
from jax.sharding import PartitionSpec as P

MODEL_WIDTH = 1024
QUERY_HEADS = 16
KEY_VALUE_HEADS = 8
HEAD_SIZE = 64
FF = 512
EXP_WIN = 1
STEP = 5
PROJ = 2048
CAP = 32


NORM_EPS = 1e-06
ROPE_BASE = 10000.0
ATTN_MULT = 0.015625
RESID_MULT = 0.22
LEARN_RATE = 0.05
BETA_ONE = 0.9
BETA_TWO = 0.95
ADAM_EPS = 1e-08
DECAY = 0.1


STREAMS = 3


def to_rows(flat_vec, offset, rows):
    room = jnp.zeros(((rows + 1) * PROJ,), flat_vec.dtype)
    return lax.dynamic_update_slice(room, flat_vec, (offset,)).reshape(rows + 1, PROJ)


def bits_of(name, count):
    return [(name, 1 << k) for k in reversed(range(count.bit_length() - 1))]


def stage_orders(rep_count, grp_count):
    dims = bits_of("rep", rep_count)[:-1] + bits_of("grp", grp_count)
    head, tail = dims[:-STREAMS], dims[-STREAMS:]
    return [head + tail[i:] + tail[:i] + [("rep", 1)] for i in range(STREAMS)]


def swap(piece, dim):
    name, bit = dim
    count = lax.axis_size(name)
    return lax.ppermute(piece, name, [(i, i ^ bit) for i in range(count)])


def my_bit(dim):
    name, bit = dim
    return (lax.axis_index(name) // bit) % 2


def gather_streams(streams, orders):
    for stage in range(len(orders[0]) - 1):
        others = [swap(piece, order[stage]) for piece, order in zip(streams, orders)]
        streams, others = lax.optimization_barrier((streams, others))
        streams = [jnp.concatenate(pair) for pair in zip(streams, others)]
    return streams, [swap(piece, order[-1]) for piece, order in zip(streams, orders)]


def add_pieces(mine, other, dtype):
    return (mine.astype(F32) + other.astype(F32)).astype(dtype)


def reduce_streams(keeps, sends, orders):
    for stage in reversed(range(len(orders[0]))):
        others = [swap(piece, order[stage]) for piece, order in zip(sends, orders)]
        keeps, others = lax.optimization_barrier((keeps, others))
        if stage == 0:
            return [add_pieces(*pair, F32)[0] for pair in zip(keeps, others)]
        half = keeps[0].shape[0] // 2
        sends = [add_pieces(m[half:], o[half:], LOW) for m, o in zip(keeps, others)]
        keeps = [add_pieces(m[:half], o[:half], LOW) for m, o in zip(keeps, others)]


class Plan:
    def __init__(self, rep_count, grp_count, rows):
        self.orders = stage_orders(rep_count, grp_count)
        self.count = rep_count * grp_count
        self.half = self.count // 2
        self.rows = rows
        self.part = rows // STREAMS
        self.core = grp_count
        self.weights = [
            [bit * grp_count if name == "rep" else bit for name, bit in order]
            for order in self.orders
        ]

    def mask(self, stream, place):
        return sum(w for k, w in enumerate(self.weights[stream]) if place >> k & 1)

    def place(self, stream, device):
        return sum(
            ((device // w) % 2) * 2**k for k, w in enumerate(self.weights[stream][:-1])
        )

    def starts(self, stream):
        return [
            (place, lambda me, m=self.mask(stream, place): (me ^ m))
            for place in range(self.count)
        ]


def order_by_device(plan, me, mine, others):
    out = []
    for stream in range(STREAMS):
        both = jnp.concatenate([mine[stream], others[stream]])
        devices = jnp.arange(plan.count, dtype=jnp.int32) ^ me
        places = plan.place(stream, devices) + plan.half * ((devices // plan.core) % 2)
        out.append(jnp.take(both, places, axis=0))
    return out


def order_by_place(plan, me, streams):
    keeps, sends = [], []
    for stream in range(STREAMS):
        masks = jnp.array([plan.mask(stream, p) for p in range(plan.count)], jnp.int32)
        both = jnp.take(streams[stream], masks ^ me, axis=0)
        keeps.append(both[: plan.half])
        sends.append(both[plan.half :])
    return keeps, sends


def rope_tables(sequence_length):
    half_width = HEAD_SIZE // 2
    frequency = ROPE_BASE ** (-(jnp.arange(half_width).astype(jnp.float32) * 2.0) / HEAD_SIZE)
    angles = jnp.arange(sequence_length).astype(jnp.float32)[:, None] * frequency[None, :]
    copies = 128 // half_width
    return jnp.tile(jnp.cos(angles), (1, copies)), jnp.tile(jnp.sin(angles), (1, copies))


F32 = jnp.float32
LOW = jnp.bfloat16
QKV_ROWS = MODEL_WIDTH + 128
OUT_ROWS = FF + 128
ALL_ROWS = MODEL_WIDTH + OUT_ROWS
QUERY_COLS = QUERY_HEADS * HEAD_SIZE
KV_COLS = KEY_VALUE_HEADS * HEAD_SIZE


def mm(a, b):
    return lax.dot_general(a, b, (((1,), (0,)), ((), ())), preferred_element_type=F32)


def mm_nt(a, b):
    return lax.dot_general(a, b, (((1,), (1,)), ((), ())), preferred_element_type=F32)


def mm_tn(a, b):
    return lax.dot_general(a, b, (((0,), (0,)), ((), ())), preferred_element_type=F32)


def lanes(shape):
    return lax.broadcasted_iota(jnp.int32, shape, len(shape) - 1)


def shift_in(values):
    room = jnp.zeros((values.shape[0], 128), values.dtype)
    return pltpu.roll(jnp.concatenate([values, room], axis=1), 1, 1)


def shift_out(values):
    width = values.shape[1]
    return pltpu.roll(values, width - 1, 1)[:, : width - 128]


def turn(block, cos_table, sin_table, first):
    half = jnp.where(first, -pltpu.roll(block, 96, 1), pltpu.roll(block, 32, 1))
    return block * cos_table + half * sin_table


def turn_back(block, cos_table, sin_table, first):
    scaled = block * sin_table
    half = jnp.where(first, -pltpu.roll(scaled, 96, 1), pltpu.roll(scaled, 32, 1))
    return block * cos_table - half


def twice(block, odd, low_half):
    other = pltpu.roll(block, 64, 1)
    return jnp.where(low_half, other, block) if odd else jnp.where(low_half, block, other)


def stack_heads(block, low_half):
    zero = jnp.zeros_like(block)
    return jnp.concatenate([jnp.where(low_half, block, zero), jnp.where(low_half, zero, block)])


def forward_kernel(x_ref, main_ref, cos_ref, sin_ref, xpad_ref, q_ref, k_ref, v_ref, p_ref, att_ref):
    inputs = x_ref[...].astype(F32)
    gain = main_ref[0:16, :MODEL_WIDTH].astype(F32)[0:1]
    scale = lax.rsqrt(jnp.mean(inputs * inputs, axis=1, keepdims=True) + NORM_EPS)
    normed = (inputs * scale * gain).astype(LOW).astype(F32)
    xpad = shift_in(normed).astype(LOW)
    xpad_ref[...] = xpad
    length = inputs.shape[0]
    lane = lanes((length, 128))
    first = lane % HEAD_SIZE < HEAD_SIZE // 2
    low_half = lane < HEAD_SIZE
    cos_table = cos_ref[...]
    sin_table = sin_ref[...]
    row = lax.broadcasted_iota(jnp.int32, (2 * length, length), 0) % length
    causal = row >= lanes((2 * length, length))
    keys = mm(xpad, main_ref[:QKV_ROWS, QUERY_COLS : QUERY_COLS + KV_COLS])
    values = mm(xpad, main_ref[:QKV_ROWS, QUERY_COLS + KV_COLS :])
    v_ref[...] = values.astype(LOW)
    for pair in range(KV_COLS // 128):
        span = slice(128 * pair, 128 * pair + 128)
        turned = turn(keys[:, span], cos_table, sin_table, first)
        k_ref[:, span] = turned.astype(LOW)
        query_pair = mm(xpad, main_ref[:QKV_ROWS, 256 * pair : 256 * pair + 256])
        for odd in range(2):
            b = 2 * pair + odd
            wide = slice(128 * b, 128 * b + 128)
            block = turn(
                query_pair[:, 128 * odd : 128 * odd + 128], cos_table, sin_table, first
            ).astype(LOW)
            q_ref[:, wide] = block
            key_both = twice(turned, odd, low_half).astype(LOW)
            value_both = twice(values[:, span], odd, low_half).astype(LOW)
            scores = mm_nt(stack_heads(block, low_half), key_both) * ATTN_MULT
            scores = jnp.where(causal, scores, -jnp.inf)
            top = jnp.max(scores, axis=1, keepdims=True)
            log_total = top + jnp.log(jnp.sum(jnp.exp(scores - top), axis=1, keepdims=True))
            probs = jnp.exp(scores - log_total)
            p_ref[2 * length * b : 2 * length * (b + 1), :] = probs
            mixed = mm(probs.astype(LOW), value_both)
            att_ref[:, wide] = jnp.where(low_half, mixed[:length], mixed[length:]).astype(LOW)


def collect(plan, me, mine, others, target, semaphore, first, width):
    for stream in range(STREAMS):
        for place, device_of in plan.starts(stream):
            source = mine[stream] if place < plan.half else others[stream]
            start = device_of(me) * plan.rows + stream * plan.part
            pltpu.make_async_copy(
                source.at[place % plan.half, :, pl.ds(first, width)],
                target.at[pl.ds(pl.multiple_of(start, plan.part), plan.part), :],
                semaphore,
            ).start()


def collected(plan, target, semaphore):
    span = target.at[pl.ds(0, plan.count * plan.rows), :]
    pltpu.make_async_copy(span, span, semaphore).wait()


def gather_kernel(plan, me_ref, x_ref, cos_ref, sin_ref, *refs):
    mine, others = refs[:STREAMS], refs[STREAMS : 2 * STREAMS]
    main_ref = refs[2 * STREAMS]
    results = refs[2 * STREAMS + 1 : -4]
    tail_low, tail_tiles, semaphore, tail_semaphore = refs[-4:]
    me = me_ref[0]
    collect(plan, me, mine, others, main_ref, semaphore, 0, PROJ)
    first = PROJ + MODEL_WIDTH
    tail_copies = [
        pltpu.make_async_copy(
            source.at[:, :, pl.ds(first, 128)],
            tail_low.at[pl.ds(i * plan.half, plan.half)],
            tail_semaphore.at[i],
        )
        for i, source in enumerate((mine[0], others[0]))
    ]
    for copy in tail_copies:
        copy.start()
    spare = plan.count * plan.rows
    main_ref[spare:, :] = jnp.zeros((ALL_ROWS - spare, PROJ), LOW)
    for copy in tail_copies:
        copy.wait()
    tail_tiles[...] = tail_low[...].astype(F32).reshape(tail_tiles.shape)
    wide = jnp.concatenate(
        [tail_tiles[pl.ds(r, plan.count, stride=plan.part), :] for r in range(plan.part)], axis=1
    )
    collected(plan, main_ref, semaphore)
    top = lax.broadcasted_iota(jnp.int32, (plan.part, PROJ), 0) == 0
    for place, device_of in plan.starts(0):
        start = pl.multiple_of((device_of(me) + 1) * plan.rows, plan.part)
        extra = jnp.where(top, wide[place : place + 1], 0.0).astype(LOW)
        main_ref[pl.ds(start, plan.part), :] = main_ref[pl.ds(start, plan.part), :] + extra
    forward_kernel(x_ref, main_ref, cos_ref, sin_ref, *results)


def split_matrix():
    r = lax.broadcasted_iota(jnp.int32, (256, 256), 0)
    c = lax.broadcasted_iota(jnp.int32, (256, 256), 1)
    return (r == 2 * (c % 128) + c // 128).astype(F32).astype(LOW)


def pick(onehot, table):
    high = table.astype(LOW)
    rest = (table - high.astype(F32)).astype(LOW)
    return mm(onehot, high) + mm(onehot, rest)


def gather_expert_kernel(plan, me_ref, *refs):
    streams = refs[7 : 7 + 2 * STREAMS]
    weights, semaphore = refs[-2:]
    first = PROJ
    collect(
        plan, me_ref[0], streams[:STREAMS], streams[STREAMS:], weights, semaphore, first, MODEL_WIDTH
    )

    def ready():
        collected(plan, weights, semaphore)

    expert_kernel(*refs[:7], weights, *refs[7 + 2 * STREAMS : -2], ready=ready)


def expert_kernel(
    x_ref, cot_ref, index_ref, gate_ref, att_ref, gain_ref, wout_ref, wexp_ref,
    out_ref, grad_hidden_ref, grad_att_ref, grad_exp_ref, grad_out_ref, grad_gain_ref,
    ready=lambda: None,
):
    inputs = x_ref[...].astype(F32)
    length = inputs.shape[0]
    cot = cot_ref[...]
    gain = gain_ref[0:16, MODEL_WIDTH:].astype(F32)[0:1]
    split = split_matrix()
    halves = [mm(att_ref[:, 256 * i : 256 * i + 256], split) for i in range(QUERY_COLS // 256)]
    even = shift_in(jnp.concatenate([h[:, :128] for h in halves], axis=1)).astype(LOW)
    odd = shift_in(jnp.concatenate([h[:, 128:] for h in halves], axis=1)).astype(LOW)
    branch = mm(even, wout_ref[:, :MODEL_WIDTH]) + mm(odd, wout_ref[:, MODEL_WIDTH:])
    hidden = inputs + RESID_MULT * branch
    scale = lax.rsqrt(jnp.mean(hidden * hidden, axis=1, keepdims=True) + NORM_EPS)
    normed = (hidden * scale * gain).astype(LOW)
    match = index_ref[...] == 0
    member = jnp.sum(jnp.where(match, 1.0, 0.0), axis=1, keepdims=True)
    weight = jnp.sum(jnp.where(match, gate_ref[...], 0.0), axis=1, keepdims=True)
    r = lax.broadcasted_iota(jnp.int32, (length, length), 0)
    below = jnp.where(r >= lanes((length, length)), 1.0, 0.0).astype(LOW)
    position = mm(below, jnp.broadcast_to(member, (length, 128)).astype(LOW))[:, :CAP] - 1.0
    slots = lanes((length, CAP)).astype(F32)
    onehot = jnp.where((position == slots) & (member > 0.0), 1.0, 0.0).astype(LOW)
    blocks = mm_tn(onehot, normed).astype(LOW)
    ready()
    gate_up = mm(blocks, wexp_ref[:MODEL_WIDTH, :])
    gate_part = gate_up[:, :FF]
    up_part = gate_up[:, FF:]
    sigma = jax.nn.sigmoid(gate_part)
    activated = (gate_part * sigma * up_part).astype(LOW)
    w_down = wexp_ref[MODEL_WIDTH:, :]
    expert_out = mm(activated, w_down)
    out_ref[...] = hidden + RESID_MULT * (weight * pick(onehot, expert_out))
    grad_blocks = mm_tn(onehot, (weight * (RESID_MULT * cot)).astype(LOW)).astype(LOW)
    grad_exp_ref[MODEL_WIDTH:, :] = mm_tn(activated, grad_blocks).astype(LOW)
    grad_act = mm_nt(grad_blocks, w_down)
    slope = sigma * (1.0 + gate_part * (1.0 - sigma))
    grad_gate_up = jnp.concatenate(
        [grad_act * up_part * slope, grad_act * gate_part * sigma], axis=1
    ).astype(LOW)
    grad_exp_ref[:MODEL_WIDTH, :] = mm_tn(blocks, grad_gate_up).astype(LOW)
    grad_normed = pick(onehot, mm_nt(grad_gate_up, wexp_ref[:MODEL_WIDTH, :]))
    grad_gain_ref[...] = jnp.sum(grad_normed * hidden * scale, axis=0, keepdims=True)
    weighted = grad_normed * gain
    inner = jnp.mean(weighted * hidden, axis=1, keepdims=True)
    grad_hidden = cot + (scale * weighted - hidden * (scale * scale * scale) * inner)
    grad_hidden_ref[...] = grad_hidden
    grad_branch = (RESID_MULT * grad_hidden).astype(LOW)
    grad_out_ref[:, :MODEL_WIDTH] = mm_tn(even, grad_branch)
    grad_out_ref[:, MODEL_WIDTH:] = mm_tn(odd, grad_branch)
    grad_even = shift_out(mm_nt(grad_branch, wout_ref[:, :MODEL_WIDTH])).astype(LOW)
    grad_odd = shift_out(mm_nt(grad_branch, wout_ref[:, MODEL_WIDTH:])).astype(LOW)
    for i in range(QUERY_COLS // 256):
        span = slice(128 * i, 128 * i + 128)
        both = jnp.concatenate([grad_even[:, span], grad_odd[:, span]], axis=1)
        grad_att_ref[:, 256 * i : 256 * i + 256] = mm_nt(both, split).astype(LOW)


def backward_kernel(
    x_ref, xpad_ref, q_ref, k_ref, v_ref, p_ref, att_ref, grad_att_ref, grad_hidden_ref,
    grad_gain_ref, grad_out_ref, main_ref, cos_ref, sin_ref,
    grad_main_ref, grad_x_ref, grad_qkv_ref,
):
    inputs = x_ref[...].astype(F32)
    length = inputs.shape[0]
    lane = lanes((length, 128))
    first = lane % HEAD_SIZE < HEAD_SIZE // 2
    low_half = lane < HEAD_SIZE
    cos_table = cos_ref[...]
    sin_table = sin_ref[...]
    for pair in range(KV_COLS // 128):
        span = slice(128 * pair, 128 * pair + 128)
        key_block = k_ref[:, span].astype(F32)
        value_block = v_ref[:, span].astype(F32)
        grad_keys, grad_values = [], []
        for odd in range(2):
            b = 2 * pair + odd
            wide = slice(128 * b, 128 * b + 128)
            key_both = twice(key_block, odd, low_half).astype(LOW)
            value_both = twice(value_block, odd, low_half).astype(LOW)
            grad_block = grad_att_ref[:, wide]
            grads = stack_heads(grad_block, low_half)
            product = grad_block.astype(F32) * att_ref[:, wide].astype(F32)
            delta = jnp.sum(stack_heads(product, low_half), axis=1, keepdims=True)
            probs = p_ref[2 * length * b : 2 * length * (b + 1), :]
            grad_scores = (probs * (mm_nt(grads, value_both) - delta) * ATTN_MULT).astype(LOW)
            value_sum = mm_tn(probs.astype(LOW), grads)
            grad_values.append(value_sum + pltpu.roll(value_sum, 64, 1))
            mixed = mm(grad_scores, key_both)
            grad_query = jnp.where(low_half, mixed[:length], mixed[length:])
            grad_qkv_ref[:, wide] = turn_back(grad_query, cos_table, sin_table, first).astype(LOW)
            key_sum = mm_tn(grad_scores, stack_heads(q_ref[:, wide], low_half))
            grad_keys.append(key_sum + pltpu.roll(key_sum, 64, 1))
        grad_key = jnp.where(low_half, grad_keys[0], grad_keys[1])
        start = QUERY_COLS + 128 * pair
        grad_qkv_ref[:, start : start + 128] = turn_back(
            grad_key, cos_table, sin_table, first
        ).astype(LOW)
        start = start + KV_COLS
        grad_qkv_ref[:, start : start + 128] = jnp.where(
            low_half, grad_values[0], grad_values[1]
        ).astype(LOW)
    xpad = xpad_ref[...]
    grad_normed = shift_out(mm_nt(grad_qkv_ref[...], main_ref[...]))
    gain = main_ref[0:16, :MODEL_WIDTH].astype(F32)[0:1]
    scale = lax.rsqrt(jnp.mean(inputs * inputs, axis=1, keepdims=True) + NORM_EPS)
    gain_grad = jnp.sum(grad_normed * inputs * scale, axis=0, keepdims=True)
    weighted = grad_normed * gain
    inner = jnp.mean(weighted * inputs, axis=1, keepdims=True)
    grad_x_ref[...] = grad_hidden_ref[...] + (
        scale * weighted - inputs * (scale * scale * scale) * inner
    )
    gains = jnp.concatenate([gain_grad, grad_gain_ref[...]], axis=1)
    grad_main_ref[QKV_ROWS:, :] = grad_out_ref[128:, :].astype(LOW)
    step = QKV_ROWS // 3
    grad_qkv = grad_qkv_ref[...]
    for i in range(3):
        part = mm_tn(xpad[:, step * i : step * (i + 1)], grad_qkv)
        if i == 0:
            top = part[:16]
            top = jnp.where(lax.broadcasted_iota(jnp.int32, top.shape, 0) == 0, gains, top)
            grad_main_ref[:16, :] = top.astype(LOW)
            grad_main_ref[16:step, :] = part[16:].astype(LOW)
        elif i == 1:
            grad_main_ref[step : 2 * step, :] = part.astype(LOW)
        else:
            over = MODEL_WIDTH - 2 * step
            grad_main_ref[2 * step : MODEL_WIDTH, :] = part[:over].astype(LOW)
            grad_main_ref[MODEL_WIDTH:QKV_ROWS, :] = (part[over:] + grad_out_ref[:128, :]).astype(
                LOW
            )


def spread(plan, me, source, keeps, sends, semaphores, first, width):
    mine = (me // plan.core) % 2
    for stream in range(STREAMS):
        shift = plan.place(stream, me)
        for base in range(plan.count):
            if base // plan.core % 2:
                continue
            place = plan.place(stream, base) ^ shift
            for i, targets in enumerate((keeps, sends)):
                device = base + plan.core * (mine if i == 0 else 1 - mine)
                start = device * plan.rows + stream * plan.part
                pltpu.make_async_copy(
                    source.at[pl.ds(pl.multiple_of(start, plan.part), plan.part), :],
                    targets[stream].at[place, :, pl.ds(first, width)],
                    semaphores.at[i, stream],
                ).start()


def spread_done(plan, keeps, sends, semaphores, first, width):
    for stream in range(STREAMS):
        for i, targets in enumerate((keeps, sends)):
            span = targets[stream].at[:, :, pl.ds(first, width)]
            pltpu.make_async_copy(span, span, semaphores.at[i, stream]).wait()


def scatter_kernel(plan, me_ref, grad_exp_ref, *refs):
    inputs = refs[:14]
    grad_x_ref = refs[14]
    keeps, sends = refs[15 : 15 + STREAMS], refs[15 + STREAMS : 15 + 2 * STREAMS]
    grad_qkv_ref, grad_main_ref, tail_tiles, tail_low, exp_sems, main_sems, tail_sems = refs[-7:]
    me = me_ref[0]
    spread(plan, me, grad_exp_ref, keeps, sends, exp_sems, PROJ, MODEL_WIDTH)
    backward_kernel(*inputs, grad_main_ref, grad_x_ref, grad_qkv_ref)
    spread(plan, me, grad_main_ref, keeps, sends, main_sems, 0, PROJ)
    picked = jnp.concatenate(
        [
            grad_main_ref[plan.rows * d : plan.rows * d + plan.part, :].astype(F32)[:1]
            for d in range(1, plan.count + 1)
        ]
    )
    for r in range(plan.part):
        tail_tiles[pl.ds(r, plan.count, stride=plan.part), :] = picked[:, 128 * r : 128 * r + 128]
    tail_low[...] = tail_tiles[...].astype(LOW)
    mine = (me // plan.core) % 2
    first = PROJ + MODEL_WIDTH
    shift = plan.place(0, me)
    for base in range(plan.count):
        if base // plan.core % 2:
            continue
        place = plan.place(0, base) ^ shift
        for i, target in enumerate((keeps[0], sends[0])):
            device = base + plan.core * (mine if i == 0 else 1 - mine)
            start = pl.multiple_of(device * plan.part, plan.part)
            pltpu.make_async_copy(
                tail_low.at[pl.ds(start, plan.part), :],
                target.at[place, :, pl.ds(first, 128)],
                tail_sems.at[i],
            ).start()
    spread_done(plan, keeps, sends, exp_sems, PROJ, MODEL_WIDTH)
    spread_done(plan, keeps, sends, main_sems, 0, PROJ)
    for i, target in enumerate((keeps[0], sends[0])):
        span = target.at[:, :, pl.ds(first, 128)]
        pltpu.make_async_copy(span, span, tail_sems.at[i]).wait()


def whole(shape):
    return pl.BlockSpec(shape, lambda i: (0,) * len(shape))


ANYWHERE = pl.BlockSpec(memory_space=pl.ANY)
SCALARS = pl.BlockSpec(memory_space=pltpu.SMEM)


def call(body, outs, args, specs=None, scratch=(), out_specs=None):
    specs = specs or {}
    out_specs = out_specs or {}
    return pl.pallas_call(
        body,
        grid=(1,),
        in_specs=[specs.get(i, whole(a.shape)) for i, a in enumerate(args)],
        out_specs=[out_specs.get(i, whole(s)) for i, (s, _) in enumerate(outs)],
        out_shape=[jax.ShapeDtypeStruct(s, d) for s, d in outs],
        scratch_shapes=list(scratch),
        compiler_params=pltpu.CompilerParams(vmem_limit_bytes=VMEM_LIMIT),
    )(*args)


VMEM_LIMIT = 48 * 1024 * 1024


def layer(plan, me, tokens, cotangent, expert_index, gate_weight, mine, others):
    length = tokens.shape[0]
    cos_table, sin_table = rope_tables(length)
    aligned = plan.part % 16 == 0
    me_row = me.astype(jnp.int32).reshape(1)
    streams = (*mine, *others)
    total = plan.count * plan.rows
    qkv_spec = pl.BlockSpec((QKV_ROWS, PROJ), lambda i: (0, 0))
    forward_outs = [
        ((length, QKV_ROWS), LOW),
        ((length, QUERY_COLS), LOW),
        ((length, KV_COLS), LOW),
        ((length, KV_COLS), LOW),
        ((QUERY_HEADS * length, length), F32),
        ((length, QUERY_COLS), LOW),
    ]
    if aligned:
        main, *saved = call(
            partial(gather_kernel, plan),
            [((ALL_ROWS, PROJ), LOW)] + forward_outs,
            (me_row, tokens, cos_table, sin_table, *streams),
            {0: SCALARS, **{4 + i: ANYWHERE for i in range(2 * STREAMS)}},
            (
                pltpu.VMEM((plan.count, plan.part, 128), LOW),
                pltpu.VMEM((plan.count * plan.part, 128), F32),
                pltpu.SemaphoreType.DMA,
                pltpu.SemaphoreType.DMA((2,)),
            ),
        )
    else:
        main, experts = assemble(plan, me, mine, others)
        saved = call(
            forward_kernel, forward_outs, (tokens, main, cos_table, sin_table), {1: qkv_spec}
        )
    xpad, query, keys, values, probs, att = saved
    wout_spec = pl.BlockSpec((pl.Element(OUT_ROWS), pl.Element(PROJ)), lambda i: (MODEL_WIDTH, 0))
    gain_spec = pl.BlockSpec((16, PROJ), lambda i: (0, 0))
    expert_outs = [
        ((length, MODEL_WIDTH), F32),
        ((length, MODEL_WIDTH), F32),
        ((length, QUERY_COLS), LOW),
        ((total, MODEL_WIDTH), LOW),
        ((OUT_ROWS, PROJ), F32),
        ((1, MODEL_WIDTH), F32),
    ]
    expert_args = (tokens, cotangent, expert_index, gate_weight, att, main, main)
    if aligned:
        results = call(
            partial(gather_expert_kernel, plan),
            expert_outs,
            (me_row, *expert_args, *streams),
            {
                0: SCALARS, 6: gain_spec, 7: wout_spec,
                **{8 + i: ANYWHERE for i in range(2 * STREAMS)},
            },
            (pltpu.VMEM((total, MODEL_WIDTH), LOW), pltpu.SemaphoreType.DMA),
        )
    else:
        results = call(
            expert_kernel, expert_outs, (*expert_args, experts), {5: gain_spec, 6: wout_spec}
        )
    output, grad_hidden, grad_att, grad_exp, grad_out, grad_gain = results
    backward_args = (
        tokens, xpad, query, keys, values, probs, att, grad_att, grad_hidden,
        grad_gain, grad_out, main, cos_table, sin_table,
    )
    if aligned:
        shapes = [(plan.half, plan.part, w) for w in stream_widths(plan)]
        grad_tokens, *pieces = call(
            partial(scatter_kernel, plan),
            [((length, MODEL_WIDTH), F32)] + [(shape, LOW) for shape in shapes + shapes],
            (me_row, grad_exp, *backward_args),
            {0: SCALARS, 13: qkv_spec},
            (
                pltpu.VMEM((length, PROJ), LOW),
                pltpu.VMEM((ALL_ROWS, PROJ), LOW),
                pltpu.VMEM((plan.count * plan.part, 128), F32),
                pltpu.VMEM((plan.count * plan.part, 128), LOW),
                pltpu.SemaphoreType.DMA((2, STREAMS)),
                pltpu.SemaphoreType.DMA((2, STREAMS)),
                pltpu.SemaphoreType.DMA((2,)),
            ),
            {1 + i: ANYWHERE for i in range(2 * STREAMS)},
        )
        return output, grad_tokens, pieces[:STREAMS], pieces[STREAMS:]
    grad_main, grad_tokens = call(
        backward_kernel,
        [((ALL_ROWS, PROJ), LOW), ((length, MODEL_WIDTH), F32)],
        backward_args,
        {11: qkv_spec},
        (pltpu.VMEM((length, PROJ), LOW),),
    )
    tails = grad_main[plan.rows : total + 1 : plan.rows].reshape(plan.count, plan.part, -1)
    windows = jnp.concatenate(
        [
            grad_main[:total].reshape(plan.count, STREAMS, plan.part, PROJ),
            grad_exp.reshape(plan.count, STREAMS, plan.part, MODEL_WIDTH),
        ],
        axis=3,
    )
    split = [jnp.concatenate([windows[:, 0], tails], axis=2)]
    split = split + [windows[:, i] for i in range(1, STREAMS)]
    return output, grad_tokens, *order_by_place(plan, me, split)


def stream_widths(plan):
    wide = PROJ + MODEL_WIDTH
    return [wide + PROJ // plan.part] + [wide] * (STREAMS - 1)


def assemble(plan, me, mine, others):
    pieces = order_by_device(plan, me, mine, others)
    total = plan.count * plan.rows
    tails = pieces[0][:, :, PROJ + MODEL_WIDTH :].reshape(plan.count, PROJ)
    main = jnp.stack([piece[:, :, :PROJ] for piece in pieces], axis=1).reshape(total, PROJ)
    main = jnp.concatenate([main, jnp.zeros((ALL_ROWS - total, PROJ), LOW)])
    main = main.at[plan.rows : total + 1 : plan.rows].add(tails)
    experts = [piece[:, :, PROJ : PROJ + MODEL_WIDTH] for piece in pieces]
    return main, jnp.stack(experts, axis=1).reshape(total, MODEL_WIDTH)


def adamw(current, gradient, moment_one, moment_two):
    moment_one_new = BETA_ONE * moment_one + (1.0 - BETA_ONE) * gradient
    moment_two_new = BETA_TWO * moment_two + (1.0 - BETA_TWO) * gradient * gradient
    first_hat = moment_one_new / (1.0 - BETA_ONE**STEP)
    second_hat = moment_two_new / (1.0 - BETA_TWO**STEP)
    updated = current - LEARN_RATE * (
        first_hat / (jnp.sqrt(second_hat) + ADAM_EPS) + DECAY * current
    )
    return (updated, moment_one_new, moment_two_new)


def per_device(
    tokens,
    cotangent,
    expert_index,
    gate_weight,
    attn_params,
    attn_first,
    attn_second,
    expert_params,
    expert_first,
    expert_second,
):
    rep_count = lax.axis_size("rep")
    grp_count = lax.axis_size("grp")
    me = lax.axis_index("rep") * grp_count + lax.axis_index("grp")
    rows = attn_params.shape[0] // PROJ
    extra = attn_params.shape[0] - rows * PROJ
    part_rows = rows // STREAMS
    attn_rows = to_rows(attn_params.astype(jnp.bfloat16), extra * me, rows)
    expert_rows = expert_params.astype(jnp.bfloat16).reshape(rows, MODEL_WIDTH)
    tail_tile = attn_rows[rows].reshape(part_rows, PROJ // part_rows)
    both = jnp.concatenate([attn_rows[:rows], expert_rows], axis=1).reshape(
        STREAMS, part_rows, PROJ + MODEL_WIDTH
    )
    streams = [jnp.concatenate([both[0], tail_tile], axis=1)] + [both[i] for i in range(1, STREAMS)]
    plan = Plan(rep_count, grp_count, rows)
    mine, others = gather_streams([piece[None] for piece in streams], plan.orders)
    output, grad_tokens, keeps, sends = layer(
        plan, me, tokens, cotangent, expert_index, gate_weight, mine, others
    )
    streams = reduce_streams(keeps, sends, plan.orders)
    tail_owned = streams[0][:, PROJ + MODEL_WIDTH :].reshape(1, PROJ)
    attn_owned = jnp.concatenate([piece[:, :PROJ] for piece in streams] + [tail_owned])
    attn_grad = lax.dynamic_slice(
        attn_owned.reshape(-1), (extra * me,), (attn_params.shape[0],)
    )
    expert_grad = jnp.concatenate(
        [piece[:, PROJ : PROJ + MODEL_WIDTH] for piece in streams]
    ).reshape(-1)
    new_attn, new_attn_first, new_attn_second = adamw(
        attn_params, attn_grad, attn_first, attn_second
    )
    new_expert, new_expert_first, new_expert_second = adamw(
        expert_params, expert_grad, expert_first, expert_second
    )
    return (
        output,
        grad_tokens,
        attn_grad,
        expert_grad,
        new_attn,
        new_attn_first,
        new_attn_second,
        new_expert,
        new_expert_first,
        new_expert_second,
    )


def solution(mesh):
    in_specs = (
        P(("rep", "grp"), None),
        P(("rep", "grp"), None),
        P(("rep", "grp"), None),
        P(("rep", "grp"), None),
        P(("rep", "grp")),
        P(("rep", "grp")),
        P(("rep", "grp")),
        P(("rep", "grp")),
        P(("rep", "grp")),
        P(("rep", "grp")),
    )
    out_specs = (
        P(("rep", "grp"), None),
        P(("rep", "grp"), None),
        P(("rep", "grp")),
        P(("rep", "grp")),
        P(("rep", "grp")),
        P(("rep", "grp")),
        P(("rep", "grp")),
        P(("rep", "grp")),
        P(("rep", "grp")),
        P(("rep", "grp")),
    )
    return jax.shard_map(
        per_device, mesh=mesh, in_specs=in_specs, out_specs=out_specs, check_vma=False
    )
```

```python
from functools import partial

import jax
import jax.numpy as jnp
from jax import lax
from jax.experimental import pallas as pl
from jax.experimental.pallas import tpu as pltpu
from jax.sharding import PartitionSpec as P

MODEL_WIDTH = 1024
QUERY_HEADS = 16
KEY_VALUE_HEADS = 8
HEAD_SIZE = 64
FF = 512
EXP_WIN = 1
STEP = 5
PROJ = 2048
CAP = 32


NORM_EPS = 1e-06
ROPE_BASE = 10000.0
ATTN_MULT = 0.015625
RESID_MULT = 0.22
LEARN_RATE = 0.05
BETA_ONE = 0.9
BETA_TWO = 0.95
ADAM_EPS = 1e-08
DECAY = 0.1


STREAMS = 3


def to_rows(flat_vec, offset, rows):
    room = jnp.zeros(((rows + 1) * PROJ,), flat_vec.dtype)
    return lax.dynamic_update_slice(room, flat_vec, (offset,)).reshape(rows + 1, PROJ)


def bits_of(name, count):
    return [(name, 1 << k) for k in reversed(range(count.bit_length() - 1))]


def stage_orders(rep_count, grp_count):
    dims = bits_of("rep", rep_count)[:-1] + bits_of("grp", grp_count)
    head, tail = dims[:-STREAMS], dims[-STREAMS:]
    return [head + tail[i:] + tail[:i] + [("rep", 1)] for i in range(STREAMS)]


def swap(piece, dim):
    name, bit = dim
    count = lax.axis_size(name)
    return lax.ppermute(piece, name, [(i, i ^ bit) for i in range(count)])


def my_bit(dim):
    name, bit = dim
    return (lax.axis_index(name) // bit) % 2


def after(pieces, *events):
    return lax.optimization_barrier((pieces, events))[0]


def swap_all(streams, orders, stage):
    dims = [order[stage] for order in orders]
    if streams[0].shape[0] > 1 or len(set(dims)) > 1:
        return [swap(piece, dim) for piece, dim in zip(streams, dims)]
    widths = [piece.shape[-1] for piece in streams]
    joined = swap(jnp.concatenate(streams, axis=-1), dims[0])
    starts = [sum(widths[:i]) for i in range(len(widths))]
    return [joined[..., start : start + width] for start, width in zip(starts, widths)]


def grow(streams, orders, stage):
    others = swap_all(streams, orders, stage)
    streams, others = lax.optimization_barrier((streams, others))
    return [jnp.concatenate(pair) for pair in zip(streams, others)]


def add_pieces(mine, other, dtype):
    return (mine.astype(F32) + other.astype(F32)).astype(dtype)


def halve(keeps, others):
    keeps, others = lax.optimization_barrier((keeps, others))
    half = keeps[0].shape[0] // 2
    sends = [add_pieces(m[half:], o[half:], LOW) for m, o in zip(keeps, others)]
    keeps = [add_pieces(m[:half], o[:half], LOW) for m, o in zip(keeps, others)]
    return keeps, sends


def join(attn, expert):
    return [jnp.concatenate(pair, axis=-1) for pair in zip(attn, expert)]


class Plan:
    def __init__(self, rep_count, grp_count, rows):
        self.orders = stage_orders(rep_count, grp_count)
        self.count = rep_count * grp_count
        self.half = self.count // 2
        self.quarter = self.count // 4
        self.rows = rows
        self.part = rows // STREAMS
        self.core = grp_count
        self.weights = [
            [bit * grp_count if name == "rep" else bit for name, bit in order]
            for order in self.orders
        ]

    def mask(self, stream, place):
        return sum(w for k, w in enumerate(self.weights[stream]) if place >> k & 1)

    def place(self, stream, device):
        return sum(
            ((device // w) % 2) * 2**k for k, w in enumerate(self.weights[stream][:-1])
        )

    def starts(self, stream):
        return [
            (place, lambda me, m=self.mask(stream, place): (me ^ m))
            for place in range(self.count)
        ]


def order_by_device(plan, me, groups):
    out = []
    for stream in range(STREAMS):
        both = jnp.concatenate([group[stream] for group in groups])
        devices = jnp.arange(plan.count, dtype=jnp.int32) ^ me
        places = plan.place(stream, devices) + plan.half * ((devices // plan.core) % 2)
        out.append(jnp.take(both, places, axis=0))
    return out


def order_by_place(plan, me, streams):
    keeps, sends = [], []
    for stream in range(STREAMS):
        masks = jnp.array([plan.mask(stream, p) for p in range(plan.count)], jnp.int32)
        both = jnp.take(streams[stream], masks ^ me, axis=0)
        keeps.append(both[: plan.half])
        sends.append(both[plan.half :])
    return keeps, sends


def rope_tables(sequence_length):
    half_width = HEAD_SIZE // 2
    frequency = ROPE_BASE ** (-(jnp.arange(half_width).astype(jnp.float32) * 2.0) / HEAD_SIZE)
    angles = jnp.arange(sequence_length).astype(jnp.float32)[:, None] * frequency[None, :]
    copies = 128 // half_width
    return jnp.tile(jnp.cos(angles), (1, copies)), jnp.tile(jnp.sin(angles), (1, copies))


F32 = jnp.float32
LOW = jnp.bfloat16
QKV_ROWS = MODEL_WIDTH + 128
OUT_ROWS = FF + 128
ALL_ROWS = MODEL_WIDTH + OUT_ROWS
QUERY_COLS = QUERY_HEADS * HEAD_SIZE
KV_COLS = KEY_VALUE_HEADS * HEAD_SIZE


def mm(a, b):
    return lax.dot_general(a, b, (((1,), (0,)), ((), ())), preferred_element_type=F32)


def mm_nt(a, b):
    return lax.dot_general(a, b, (((1,), (1,)), ((), ())), preferred_element_type=F32)


def mm_tn(a, b):
    return lax.dot_general(a, b, (((0,), (0,)), ((), ())), preferred_element_type=F32)


def lanes(shape):
    return lax.broadcasted_iota(jnp.int32, shape, len(shape) - 1)


def shift_in(values):
    room = jnp.zeros((values.shape[0], 128), values.dtype)
    return pltpu.roll(jnp.concatenate([values, room], axis=1), 1, 1)


def shift_out(values):
    width = values.shape[1]
    return pltpu.roll(values, width - 1, 1)[:, : width - 128]


def turn(block, cos_table, sin_table, first):
    half = jnp.where(first, -pltpu.roll(block, 96, 1), pltpu.roll(block, 32, 1))
    return block * cos_table + half * sin_table


def turn_back(block, cos_table, sin_table, first):
    scaled = block * sin_table
    half = jnp.where(first, -pltpu.roll(scaled, 96, 1), pltpu.roll(scaled, 32, 1))
    return block * cos_table - half


def twice(block, odd, low_half):
    other = pltpu.roll(block, 64, 1)
    return jnp.where(low_half, other, block) if odd else jnp.where(low_half, block, other)


def stack_heads(block, low_half):
    zero = jnp.zeros_like(block)
    return jnp.concatenate([jnp.where(low_half, block, zero), jnp.where(low_half, zero, block)])


def forward_kernel(x_ref, main_ref, cos_ref, sin_ref, xpad_ref, q_ref, k_ref, v_ref, p_ref, att_ref):
    inputs = x_ref[...].astype(F32)
    gain = main_ref[0:16, :MODEL_WIDTH].astype(F32)[0:1]
    scale = lax.rsqrt(jnp.mean(inputs * inputs, axis=1, keepdims=True) + NORM_EPS)
    normed = (inputs * scale * gain).astype(LOW).astype(F32)
    xpad = shift_in(normed).astype(LOW)
    xpad_ref[...] = xpad
    length = inputs.shape[0]
    lane = lanes((length, 128))
    first = lane % HEAD_SIZE < HEAD_SIZE // 2
    low_half = lane < HEAD_SIZE
    cos_table = cos_ref[...]
    sin_table = sin_ref[...]
    row = lax.broadcasted_iota(jnp.int32, (2 * length, length), 0) % length
    causal = row >= lanes((2 * length, length))
    keys = mm(xpad, main_ref[:QKV_ROWS, QUERY_COLS : QUERY_COLS + KV_COLS])
    values = mm(xpad, main_ref[:QKV_ROWS, QUERY_COLS + KV_COLS :])
    v_ref[...] = values.astype(LOW)
    for pair in range(KV_COLS // 128):
        span = slice(128 * pair, 128 * pair + 128)
        turned = turn(keys[:, span], cos_table, sin_table, first)
        k_ref[:, span] = turned.astype(LOW)
        query_pair = mm(xpad, main_ref[:QKV_ROWS, 256 * pair : 256 * pair + 256])
        for odd in range(2):
            b = 2 * pair + odd
            wide = slice(128 * b, 128 * b + 128)
            block = turn(
                query_pair[:, 128 * odd : 128 * odd + 128], cos_table, sin_table, first
            ).astype(LOW)
            q_ref[:, wide] = block
            key_both = twice(turned, odd, low_half).astype(LOW)
            value_both = twice(values[:, span], odd, low_half).astype(LOW)
            scores = mm_nt(stack_heads(block, low_half), key_both) * ATTN_MULT
            scores = jnp.where(causal, scores, -jnp.inf)
            top = jnp.max(scores, axis=1, keepdims=True)
            log_total = top + jnp.log(jnp.sum(jnp.exp(scores - top), axis=1, keepdims=True))
            probs = jnp.exp(scores - log_total)
            p_ref[2 * length * b : 2 * length * (b + 1), :] = probs
            mixed = mm(probs.astype(LOW), value_both)
            att_ref[:, wide] = jnp.where(low_half, mixed[:length], mixed[length:]).astype(LOW)


def grouped(refs):
    return [refs[STREAMS * i : STREAMS * (i + 1)] for i in range(4)]


def collect(plan, me, groups, target, width):
    for stream in range(STREAMS):
        for place, device_of in plan.starts(stream):
            source = groups[place // plan.quarter][stream]
            start = device_of(me) * plan.rows + stream * plan.part
            start = pl.multiple_of(start, plan.part)
            target[pl.ds(start, plan.part), :] = source[place % plan.quarter, :, :width]


def gather_kernel(plan, me_ref, x_ref, cos_ref, sin_ref, *refs):
    groups = grouped(refs)
    main_ref = refs[4 * STREAMS]
    results = refs[4 * STREAMS + 1 : -1]
    tail_tiles = refs[-1]
    me = me_ref[0]
    collect(plan, me, groups, main_ref, PROJ)
    spare = plan.count * plan.rows
    main_ref[spare:, :] = jnp.zeros((ALL_ROWS - spare, PROJ), LOW)
    size = plan.quarter * plan.part
    for i, group in enumerate(groups):
        tiles = group[0][:, :, PROJ:].astype(F32).reshape(-1, 128)
        tail_tiles[i * size : (i + 1) * size, :] = tiles
    wide = jnp.concatenate(
        [tail_tiles[pl.ds(r, plan.count, stride=plan.part), :] for r in range(plan.part)], axis=1
    )
    top = lax.broadcasted_iota(jnp.int32, (plan.part, PROJ), 0) == 0
    for place, device_of in plan.starts(0):
        start = pl.multiple_of((device_of(me) + 1) * plan.rows, plan.part)
        extra = jnp.where(top, wide[place : place + 1], 0.0).astype(LOW)
        main_ref[pl.ds(start, plan.part), :] = main_ref[pl.ds(start, plan.part), :] + extra
    forward_kernel(x_ref, main_ref, cos_ref, sin_ref, *results)


def split_matrix():
    r = lax.broadcasted_iota(jnp.int32, (256, 256), 0)
    c = lax.broadcasted_iota(jnp.int32, (256, 256), 1)
    return (r == 2 * (c % 128) + c // 128).astype(F32).astype(LOW)


def pick(onehot, table):
    high = table.astype(LOW)
    rest = (table - high.astype(F32)).astype(LOW)
    return mm(onehot, high) + mm(onehot, rest)


def route_kernel(index_ref, gate_ref, onehot_ref, weight_ref):
    length = index_ref.shape[0]
    match = index_ref[...] == 0
    member = jnp.sum(jnp.where(match, 1.0, 0.0), axis=1, keepdims=True)
    weight_ref[...] = jnp.sum(jnp.where(match, gate_ref[...], 0.0), axis=1, keepdims=True)
    r = lax.broadcasted_iota(jnp.int32, (length, length), 0)
    below = jnp.where(r >= lanes((length, length)), 1.0, 0.0).astype(LOW)
    position = mm(below, jnp.broadcast_to(member, (length, 128)).astype(LOW))[:, :CAP] - 1.0
    slots = lanes((length, CAP)).astype(F32)
    onehot = jnp.where((position == slots) & (member > 0.0), 1.0, 0.0).astype(LOW)
    onehot_ref[...] = onehot


def mix_kernel(x_ref, onehot_ref, att_ref, main_ref, hidden_ref, even_ref, odd_ref, blocks_ref):
    inputs = x_ref[...].astype(F32)
    length = inputs.shape[0]
    gain = main_ref[0:16, MODEL_WIDTH:].astype(F32)[0:1]
    split = split_matrix()
    halves = [mm(att_ref[:, 256 * i : 256 * i + 256], split) for i in range(QUERY_COLS // 256)]
    even = shift_in(jnp.concatenate([h[:, :128] for h in halves], axis=1)).astype(LOW)
    odd = shift_in(jnp.concatenate([h[:, 128:] for h in halves], axis=1)).astype(LOW)
    even_ref[...] = even
    odd_ref[...] = odd
    branch = mm(even, main_ref[MODEL_WIDTH:, :MODEL_WIDTH]) + mm(odd, main_ref[MODEL_WIDTH:, MODEL_WIDTH:])
    hidden = inputs + RESID_MULT * branch
    hidden_ref[...] = hidden
    scale = lax.rsqrt(jnp.mean(hidden * hidden, axis=1, keepdims=True) + NORM_EPS)
    normed = (hidden * scale * gain).astype(LOW)
    blocks_ref[...] = mm_tn(onehot_ref[...], normed).astype(LOW)


def gather_expert_kernel(plan, me_ref, *refs):
    groups = grouped(refs[8 : 8 + 4 * STREAMS])
    results = refs[8 + 4 * STREAMS : 13 + 4 * STREAMS]
    pieces = refs[13 + 4 * STREAMS : 13 + 6 * STREAMS]
    weights, grad_exp_ref = refs[-2:]
    me = me_ref[0]
    collect(plan, me, groups, weights, MODEL_WIDTH)
    expert_kernel(*refs[:8], weights, *results, grad_exp_ref)
    for base in range(plan.count):
        if base // plan.core % 2 == 0:
            spread(plan, me, grad_exp_ref, 0, base, pieces[:STREAMS], pieces[STREAMS:])


def expert_kernel(
    cot_ref, hidden_ref, even_ref, odd_ref, onehot_ref, weight_ref, blocks_ref, main_ref,
    wexp_ref, out_ref, grad_hidden_ref, grad_att_ref, grad_out_ref, grad_gain_ref, grad_exp_ref,
):
    cot = cot_ref[...]
    hidden = hidden_ref[...]
    even = even_ref[...]
    odd = odd_ref[...]
    onehot = onehot_ref[...]
    weight = weight_ref[...]
    blocks = blocks_ref[...]
    gain = main_ref[0:16, MODEL_WIDTH:].astype(F32)[0:1]
    split = split_matrix()
    scale = lax.rsqrt(jnp.mean(hidden * hidden, axis=1, keepdims=True) + NORM_EPS)
    grad_blocks = mm_tn(onehot, (weight * (RESID_MULT * cot)).astype(LOW)).astype(LOW)
    gate_up = mm(blocks, wexp_ref[:MODEL_WIDTH, :])
    gate_part = gate_up[:, :FF]
    up_part = gate_up[:, FF:]
    sigma = jax.nn.sigmoid(gate_part)
    activated = (gate_part * sigma * up_part).astype(LOW)
    w_down = wexp_ref[MODEL_WIDTH:, :]
    grad_exp_ref[MODEL_WIDTH:, :] = mm_tn(activated, grad_blocks).astype(LOW)
    grad_act = mm_nt(grad_blocks, w_down)
    slope = sigma * (1.0 + gate_part * (1.0 - sigma))
    grad_gate_up = jnp.concatenate(
        [grad_act * up_part * slope, grad_act * gate_part * sigma], axis=1
    ).astype(LOW)
    grad_exp_ref[:MODEL_WIDTH, :] = mm_tn(blocks, grad_gate_up).astype(LOW)
    expert_out = mm(activated, w_down)
    out_ref[...] = hidden + RESID_MULT * (weight * pick(onehot, expert_out))
    grad_normed = pick(onehot, mm_nt(grad_gate_up, wexp_ref[:MODEL_WIDTH, :]))
    grad_gain_ref[...] = jnp.sum(grad_normed * hidden * scale, axis=0, keepdims=True)
    weighted = grad_normed * gain
    inner = jnp.mean(weighted * hidden, axis=1, keepdims=True)
    grad_hidden = cot + (scale * weighted - hidden * (scale * scale * scale) * inner)
    grad_hidden_ref[...] = grad_hidden
    grad_branch = (RESID_MULT * grad_hidden).astype(LOW)
    grad_out_ref[:, :MODEL_WIDTH] = mm_tn(even, grad_branch)
    grad_out_ref[:, MODEL_WIDTH:] = mm_tn(odd, grad_branch)
    grad_even = shift_out(mm_nt(grad_branch, main_ref[MODEL_WIDTH:, :MODEL_WIDTH])).astype(LOW)
    grad_odd = shift_out(mm_nt(grad_branch, main_ref[MODEL_WIDTH:, MODEL_WIDTH:])).astype(LOW)
    for i in range(QUERY_COLS // 256):
        span = slice(128 * i, 128 * i + 128)
        both = jnp.concatenate([grad_even[:, span], grad_odd[:, span]], axis=1)
        grad_att_ref[:, 256 * i : 256 * i + 256] = mm_nt(both, split).astype(LOW)


def attention_backward_kernel(
    q_ref, k_ref, v_ref, p_ref, att_ref, grad_att_ref, cos_ref, sin_ref, grad_qkv_ref
):
    length = q_ref.shape[0]
    lane = lanes((length, 128))
    first = lane % HEAD_SIZE < HEAD_SIZE // 2
    low_half = lane < HEAD_SIZE
    cos_table = cos_ref[...]
    sin_table = sin_ref[...]
    for pair in range(KV_COLS // 128):
        span = slice(128 * pair, 128 * pair + 128)
        key_block = k_ref[:, span].astype(F32)
        value_block = v_ref[:, span].astype(F32)
        grad_keys, grad_values = [], []
        for odd in range(2):
            b = 2 * pair + odd
            wide = slice(128 * b, 128 * b + 128)
            key_both = twice(key_block, odd, low_half).astype(LOW)
            value_both = twice(value_block, odd, low_half).astype(LOW)
            grad_block = grad_att_ref[:, wide]
            grads = stack_heads(grad_block, low_half)
            product = grad_block.astype(F32) * att_ref[:, wide].astype(F32)
            delta = jnp.sum(stack_heads(product, low_half), axis=1, keepdims=True)
            probs = p_ref[2 * length * b : 2 * length * (b + 1), :]
            grad_scores = (probs * (mm_nt(grads, value_both) - delta) * ATTN_MULT).astype(LOW)
            value_sum = mm_tn(probs.astype(LOW), grads)
            grad_values.append(value_sum + pltpu.roll(value_sum, 64, 1))
            mixed = mm(grad_scores, key_both)
            grad_query = jnp.where(low_half, mixed[:length], mixed[length:])
            grad_qkv_ref[:, wide] = turn_back(grad_query, cos_table, sin_table, first).astype(LOW)
            key_sum = mm_tn(grad_scores, stack_heads(q_ref[:, wide], low_half))
            grad_keys.append(key_sum + pltpu.roll(key_sum, 64, 1))
        grad_key = jnp.where(low_half, grad_keys[0], grad_keys[1])
        start = QUERY_COLS + 128 * pair
        grad_qkv_ref[:, start : start + 128] = turn_back(
            grad_key, cos_table, sin_table, first
        ).astype(LOW)
        start = start + KV_COLS
        grad_qkv_ref[:, start : start + 128] = jnp.where(
            low_half, grad_values[0], grad_values[1]
        ).astype(LOW)


def backward_kernel(
    x_ref, xpad_ref, grad_qkv_ref, grad_hidden_ref, grad_gain_ref, grad_out_ref, main_ref,
    grad_x_ref, grad_main_ref,
):
    inputs = x_ref[...].astype(F32)
    xpad = xpad_ref[...]
    grad_normed = shift_out(mm_nt(grad_qkv_ref[...], main_ref[:QKV_ROWS, :]))
    gain = main_ref[0:16, :MODEL_WIDTH].astype(F32)[0:1]
    scale = lax.rsqrt(jnp.mean(inputs * inputs, axis=1, keepdims=True) + NORM_EPS)
    gain_grad = jnp.sum(grad_normed * inputs * scale, axis=0, keepdims=True)
    weighted = grad_normed * gain
    inner = jnp.mean(weighted * inputs, axis=1, keepdims=True)
    grad_x_ref[...] = grad_hidden_ref[...] + (
        scale * weighted - inputs * (scale * scale * scale) * inner
    )
    gains = jnp.concatenate([gain_grad, grad_gain_ref[...]], axis=1)
    step = QKV_ROWS // 3
    grad_qkv = grad_qkv_ref[...]
    for i in range(3):
        part = mm_tn(xpad[:, step * i : step * (i + 1)], grad_qkv)
        if i == 0:
            top = part[:16]
            top = jnp.where(lax.broadcasted_iota(jnp.int32, top.shape, 0) == 0, gains, top)
            grad_main_ref[:16, :] = top.astype(LOW)
            grad_main_ref[16:step, :] = part[16:].astype(LOW)
        elif i == 1:
            grad_main_ref[step : 2 * step, :] = part.astype(LOW)
        else:
            over = MODEL_WIDTH - 2 * step
            grad_main_ref[2 * step : MODEL_WIDTH, :] = part[:over].astype(LOW)
            grad_main_ref[MODEL_WIDTH:QKV_ROWS, :] = (part[over:] + grad_out_ref[:128, :]).astype(
                LOW
            )
    grad_main_ref[QKV_ROWS:, :] = grad_out_ref[128:, :].astype(LOW)


def spread_pair(mine, first, second, keep, send):
    keep_value = jnp.where(mine == 0, first, second)
    send_value = jnp.where(mine == 0, second, first)
    return (keep, keep_value), (send, send_value)


def spread(plan, me, source, offset, base, keeps, sends):
    mine = (me // plan.core) % 2
    for stream in range(STREAMS):
        place = plan.place(stream, base) ^ plan.place(stream, me)
        tiles = []
        for device in (base, base + plan.core):
            start = device * plan.rows + stream * plan.part - offset
            tiles.append(source[start : start + plan.part, :])
        width = tiles[0].shape[1]
        for ref, value in spread_pair(mine, *tiles, keeps[stream], sends[stream]):
            ref[place, :, :width] = value


def scatter_kernel(plan, me_ref, *refs):
    inputs = refs[:7]
    grad_x_ref = refs[7]
    keeps, sends = refs[8 : 8 + STREAMS], refs[8 + STREAMS : 8 + 2 * STREAMS]
    grad_main_ref, tail_tiles = refs[-2:]
    me = me_ref[0]
    backward_kernel(*inputs, grad_x_ref, grad_main_ref)
    picked = jnp.concatenate(
        [
            grad_main_ref[plan.rows * d : plan.rows * d + plan.part, :].astype(F32)[:1]
            for d in range(1, plan.count + 1)
        ]
    )
    for r in range(plan.part):
        tail_tiles[pl.ds(r, plan.count, stride=plan.part), :] = picked[:, 128 * r : 128 * r + 128]
    mine = (me // plan.core) % 2
    for base in range(plan.count):
        if base // plan.core % 2:
            continue
        spread(plan, me, grad_main_ref, 0, base, keeps, sends)
        place = plan.place(0, base) ^ plan.place(0, me)
        tiles = [
            tail_tiles[d * plan.part : (d + 1) * plan.part, :].astype(LOW)
            for d in (base, base + plan.core)
        ]
        for ref, value in spread_pair(mine, *tiles, keeps[0], sends[0]):
            ref[place, :, PROJ:] = value


INSIDE = pl.BlockSpec(memory_space=pltpu.VMEM)
SCALARS = pl.BlockSpec(memory_space=pltpu.SMEM)


def call(body, outs, args, scratch=(), scalars=0):
    return pl.pallas_call(
        body,
        in_specs=[SCALARS if i < scalars else INSIDE for i in range(len(args))],
        out_specs=[INSIDE for _ in outs],
        out_shape=[jax.ShapeDtypeStruct(s, d) for s, d in outs],
        scratch_shapes=list(scratch),
        compiler_params=pltpu.CompilerParams(vmem_limit_bytes=VMEM_LIMIT),
    )(*args)


VMEM_LIMIT = 24 * 1024 * 1024


def layer(plan, me, tokens, cotangent, expert_index, gate_weight, attn, expert):
    orders = plan.orders
    last = len(orders[0]) - 1
    length = tokens.shape[0]
    cos_table, sin_table = rope_tables(length)
    aligned = plan.part % 16 == 0
    me_row = me.astype(jnp.int32).reshape(1)
    total = plan.count * plan.rows

    onehot, weight = call(
        route_kernel,
        [((length, CAP), LOW), ((length, 1), F32)],
        (expert_index, gate_weight),
    )
    expert = grow(expert, orders, 0)
    attn = grow(attn, orders, 0)
    attn, (cos_table, sin_table, onehot, weight, tokens) = lax.optimization_barrier(
        (attn, (cos_table, sin_table, onehot, weight, tokens))
    )
    for stage in range(1, last - 1):
        attn = grow(attn, orders, stage)
    attn_late = swap_all(attn, orders, last - 1)
    attn_core = swap_all(attn, orders, last)
    expert = after(expert, attn_core)
    for stage in range(1, last - 1):
        expert = grow(expert, orders, stage)
    attn_late = after(attn_late, expert)
    attn_late_core = swap_all(attn_late, orders, last)
    expert = after(expert, attn_late)
    expert_late = swap_all(expert, orders, last - 1)
    expert_core = swap_all(expert, orders, last)
    attn_groups = (attn, attn_late, attn_core, attn_late_core)

    forward_outs = [
        ((length, QKV_ROWS), LOW),
        ((length, QUERY_COLS), LOW),
        ((length, KV_COLS), LOW),
        ((length, KV_COLS), LOW),
        ((QUERY_HEADS * length, length), F32),
        ((length, QUERY_COLS), LOW),
    ]
    if aligned:
        main, *saved = call(
            partial(gather_kernel, plan),
            [((ALL_ROWS, PROJ), LOW)] + forward_outs,
            (me_row, tokens, cos_table, sin_table, *sum(attn_groups, [])),
            (pltpu.VMEM((plan.count * plan.part, 128), F32),),
            1,
        )
    else:
        main = assemble_attn(plan, me, attn_groups)
        saved = call(forward_kernel, forward_outs, (tokens, main, cos_table, sin_table))
    xpad, query, keys, values, probs, att = saved
    expert_late = after(expert_late, att)
    expert_late_core = swap_all(expert_late, orders, last)
    expert_groups = (expert, expert_late, expert_core, expert_late_core)
    hidden, even, odd, blocks = call(
        mix_kernel,
        [
            ((length, MODEL_WIDTH), F32),
            ((length, OUT_ROWS), LOW),
            ((length, OUT_ROWS), LOW),
            ((CAP, MODEL_WIDTH), LOW),
        ],
        (after(tokens, expert_late), onehot, att, main),
    )
    expert_outs = [
        ((length, MODEL_WIDTH), F32),
        ((length, MODEL_WIDTH), F32),
        ((length, QUERY_COLS), LOW),
        ((OUT_ROWS, PROJ), F32),
        ((1, MODEL_WIDTH), F32),
    ]
    expert_args = (cotangent, hidden, even, odd, onehot, weight, blocks, main)
    if aligned:
        pieces_shape = (plan.half, plan.part, MODEL_WIDTH)
        *results, k0, k1, k2, s0, s1, s2 = call(
            partial(gather_expert_kernel, plan),
            expert_outs + [(pieces_shape, LOW)] * (2 * STREAMS),
            (me_row, *expert_args, *sum(expert_groups, [])),
            (pltpu.VMEM((total, MODEL_WIDTH), LOW), pltpu.VMEM((total, MODEL_WIDTH), LOW)),
            1,
        )
        expert_keeps, expert_sends = [k0, k1, k2], [s0, s1, s2]
    else:
        experts = assemble_expert(plan, me, expert_groups)
        *results, grad_exp = call(
            expert_kernel,
            expert_outs + [((total, MODEL_WIDTH), LOW)],
            (*expert_args, experts),
        )
        windows = grad_exp.reshape(plan.count, STREAMS, plan.part, MODEL_WIDTH)
        expert_keeps, expert_sends = order_by_place(
            plan, me, [windows[:, i] for i in range(STREAMS)]
        )
    output, grad_hidden, grad_att, grad_out, grad_gain = results
    expert_others = swap_all(expert_sends, orders, last)
    (grad_qkv,) = call(
        attention_backward_kernel,
        [((length, PROJ), LOW)],
        (query, keys, values, probs, att, after(grad_att, expert_sends), cos_table, sin_table),
    )
    expert_keeps, expert_sends = halve(expert_keeps, expert_others)
    expert_others = swap_all(expert_sends, orders, last - 1)
    grad_qkv = after(grad_qkv, expert_sends)
    backward_args = (tokens, xpad, grad_qkv, grad_hidden, grad_gain, grad_out, main)
    if aligned:
        shapes = [(plan.half, plan.part, w) for w in (PROJ + 128, PROJ, PROJ)]
        grad_tokens, k0, k1, k2, s0, s1, s2 = call(
            partial(scatter_kernel, plan),
            [((length, MODEL_WIDTH), F32)] + [(shape, LOW) for shape in shapes + shapes],
            (me_row, *backward_args),
            (
                pltpu.VMEM((ALL_ROWS, PROJ), LOW),
                pltpu.VMEM((plan.count * plan.part, 128), F32),
            ),
            1,
        )
        keeps, sends = [k0, k1, k2], [s0, s1, s2]
    else:
        grad_tokens, grad_main = call(
            backward_kernel,
            [((length, MODEL_WIDTH), F32), ((ALL_ROWS, PROJ), LOW)],
            backward_args,
        )
        tails = grad_main[plan.rows : total + 1 : plan.rows].reshape(plan.count, plan.part, -1)
        windows = grad_main[:total].reshape(plan.count, STREAMS, plan.part, PROJ)
        split = [jnp.concatenate([windows[:, 0], tails], axis=2)]
        split = split + [windows[:, i] for i in range(1, STREAMS)]
        keeps, sends = order_by_place(plan, me, split)
    others = swap_all(sends, orders, last)
    keeps, sends = halve(keeps, others)
    others = swap_all(sends, orders, last - 1)
    expert_keeps, expert_sends = halve(after(expert_keeps, sends), expert_others)
    keeps, sends = halve(keeps, others)
    keeps, sends = join(keeps, expert_keeps), join(sends, expert_sends)
    for stage in reversed(range(1, last - 1)):
        keeps, sends = halve(keeps, swap_all(sends, orders, stage))
    others = swap_all(sends, orders, 0)
    keeps, others = lax.optimization_barrier((keeps, others))
    streams = [add_pieces(m, o, F32)[0] for m, o in zip(keeps, others)]
    return output, grad_tokens, streams


def assemble_attn(plan, me, groups):
    pieces = order_by_device(plan, me, groups)
    total = plan.count * plan.rows
    tails = pieces[0][:, :, PROJ:].reshape(plan.count, PROJ)
    main = jnp.stack([piece[:, :, :PROJ] for piece in pieces], axis=1).reshape(total, PROJ)
    main = jnp.concatenate([main, jnp.zeros((ALL_ROWS - total, PROJ), LOW)])
    return main.at[plan.rows : total + 1 : plan.rows].add(tails)


def assemble_expert(plan, me, groups):
    pieces = order_by_device(plan, me, groups)
    return jnp.stack(pieces, axis=1).reshape(plan.count * plan.rows, MODEL_WIDTH)


def adamw(current, gradient, moment_one, moment_two):
    moment_one_new = BETA_ONE * moment_one + (1.0 - BETA_ONE) * gradient
    moment_two_new = BETA_TWO * moment_two + (1.0 - BETA_TWO) * gradient * gradient
    first_hat = moment_one_new / (1.0 - BETA_ONE**STEP)
    second_hat = moment_two_new / (1.0 - BETA_TWO**STEP)
    updated = current - LEARN_RATE * (
        first_hat / (jnp.sqrt(second_hat) + ADAM_EPS) + DECAY * current
    )
    return (updated, moment_one_new, moment_two_new)


def per_device(
    tokens,
    cotangent,
    expert_index,
    gate_weight,
    attn_params,
    attn_first,
    attn_second,
    expert_params,
    expert_first,
    expert_second,
):
    rep_count = lax.axis_size("rep")
    grp_count = lax.axis_size("grp")
    me = lax.axis_index("rep") * grp_count + lax.axis_index("grp")
    rows = attn_params.shape[0] // PROJ
    extra = attn_params.shape[0] - rows * PROJ
    part_rows = rows // STREAMS
    attn_rows = to_rows(attn_params.astype(jnp.bfloat16), extra * me, rows)
    expert_rows = expert_params.astype(jnp.bfloat16).reshape(rows, MODEL_WIDTH)
    tail_tile = attn_rows[rows].reshape(part_rows, PROJ // part_rows)
    expert_pieces = expert_rows.reshape(STREAMS, 1, part_rows, MODEL_WIDTH)
    attn_pieces = attn_rows[:rows].reshape(STREAMS, 1, part_rows, PROJ)
    first_piece = jnp.concatenate([attn_pieces[0], tail_tile[None]], axis=2)
    plan = Plan(rep_count, grp_count, rows)
    output, grad_tokens, streams = layer(
        plan,
        me,
        tokens,
        cotangent,
        expert_index,
        gate_weight,
        [first_piece] + [attn_pieces[i] for i in range(1, STREAMS)],
        [expert_pieces[i] for i in range(STREAMS)],
    )
    tail_owned = streams[0][:, PROJ:-MODEL_WIDTH].reshape(1, PROJ)
    attn_owned = jnp.concatenate([piece[:, :PROJ] for piece in streams] + [tail_owned])
    attn_grad = lax.dynamic_slice(
        attn_owned.reshape(-1), (extra * me,), (attn_params.shape[0],)
    )
    expert_grad = jnp.concatenate([piece[:, -MODEL_WIDTH:] for piece in streams]).reshape(-1)
    new_attn, new_attn_first, new_attn_second = adamw(
        attn_params, attn_grad, attn_first, attn_second
    )
    new_expert, new_expert_first, new_expert_second = adamw(
        expert_params, expert_grad, expert_first, expert_second
    )
    return (
        output,
        grad_tokens,
        attn_grad,
        expert_grad,
        new_attn,
        new_attn_first,
        new_attn_second,
        new_expert,
        new_expert_first,
        new_expert_second,
    )


def solution(mesh):
    in_specs = (
        P(("rep", "grp"), None),
        P(("rep", "grp"), None),
        P(("rep", "grp"), None),
        P(("rep", "grp"), None),
        P(("rep", "grp")),
        P(("rep", "grp")),
        P(("rep", "grp")),
        P(("rep", "grp")),
        P(("rep", "grp")),
        P(("rep", "grp")),
    )
    out_specs = (
        P(("rep", "grp"), None),
        P(("rep", "grp"), None),
        P(("rep", "grp")),
        P(("rep", "grp")),
        P(("rep", "grp")),
        P(("rep", "grp")),
        P(("rep", "grp")),
        P(("rep", "grp")),
        P(("rep", "grp")),
        P(("rep", "grp")),
    )
    return jax.shard_map(
        per_device, mesh=mesh, in_specs=in_specs, out_specs=out_specs, check_vma=False
    )
```
